32 devices in a mesh: groups: 2 (over y), row: 4 (over x, core), col: 4 (over z).
Axes of the slice: x: 2, y: 2, z: 4, core: 2. Of those that a mesh axis runs over, the one named last changes fastest.
Arguments:
- single: bfloat16 [512, 768], P(('groups', 'row'), 'col'), parts along dimension 0, may hold values from -16 to 16
- pair: bfloat16 [512, 256, 128], P(('groups', 'row'), 'col'), parts along dimension 0, may hold values from -6 to 6
- chain: int32 [512], P('groups'), parts along dimension 0, may hold values from 0 to 7, never falling along the last dimension, each value on 1 to 64 neighbouring positions
- live: int32 [512], P('groups'), parts along dimension 0, may hold values 0 or 1
- step_index: int32 [2], P('groups'), parts along dimension 0, may hold values from 0 to 999
- time_scale: bfloat16 [256, 768], P(None, 'col'), may hold values from -0.375 to 0.375
- time_shift: bfloat16 [256, 768], P(None, 'col'), may hold values from -0.375 to 0.375
- w_query: bfloat16 [768, 768], P(None, 'col'), may hold values from -0.21875 to 0.21875
- w_key: bfloat16 [768, 768], P(None, 'col'), may hold values from -0.21875 to 0.21875
- w_value: bfloat16 [768, 768], P(None, 'col'), may hold values from -0.21875 to 0.21875
- w_gate: bfloat16 [768, 768], P(None, 'col'), may hold values from -0.21875 to 0.21875
- w_out: bfloat16 [768, 768], P(None, 'col'), may hold values from -0.21875 to 0.21875
- pair_gain: float32 [128], replicated, may hold values from 0.1 to 1.9
- bias_weight: bfloat16 [128, 12], replicated, may hold values from -30 to 30
- chain_bias: float32 [2, 12], replicated, may hold values from -4 to 4
- outer_gain: float32 [768], P('col'), may hold values from 0.1 to 1.9
- w_left: float32 [768, 32], P('col'), may hold values from -0.21875 to 0.21875
- w_right: float32 [768, 32], P('col'), may hold values from -0.21875 to 0.21875
- w_outer: bfloat16 [32, 32, 128], replicated, may hold values from -0.1875 to 0.1875
- outer_bias: float32 [128], replicated, may hold values from -4 to 4
- trans_gain: float32 [128], replicated, may hold values from 0.1 to 1.9
- w_in: bfloat16 [128, 1024], replicated, may hold values from -0.5 to 0.5
- w_down: bfloat16 [512, 128], replicated, may hold values from -0.25 to 0.25
Outputs:
- single_out: bfloat16 [512, 768], P(('groups', 'row'), 'col'), parts along dimension 0
- pair_out: bfloat16 [512, 256, 128], P(('groups', 'row'), 'col'), parts along dimension 0
The draws below stay inside these ranges and needn't reach their ends.
There are 2 independent parts, one for each index of `groups`. The reference program is written for one: setup_inputs(seed, part) draws one part's arguments, and reference() takes and returns one part's arrays. A program takes and returns all parts, laid end to end along the dimension named above; an argument that names none is the same for every part. Nothing has to cross between parts.
Inputs may be any that keep to these rules, and one draw needn't show every extreme that they name: chain numbers never fall along the residues.
All inputs are finite; a program needn't handle non-finite values.
Results may differ from the reference program's by a relative error of at most 0.0095.
Values may be sent and summed in bfloat16 or wider, within the bound.
A program may use at most 64 MiB of HBM per device.

```python
import math
import jax
import jax.numpy as jnp
import numpy as np
from jax import lax

RB = 64
CS = 768
HEADS = 12
HD = 64
CZ = 128
HID = 512
OPM = 32
TFREQ = 256
TSTEPS = 1000
CHAINS = 8
RES = 256


def draw_single(key, part):
    key_base, key_rough = jax.random.split(jax.random.fold_in(key, 11), 2)
    base = jax.random.normal(key_base, (RES, CS), jnp.float32)
    ramp = jnp.exp(jnp.linspace(jnp.log(0.5), jnp.log(2.0), CS))
    rough = jax.random.uniform(key_rough, (CS,), jnp.float32, 0.6, 1.6)
    values = base * ramp * rough
    return jnp.clip(values, -16.0, 16.0).astype(jnp.bfloat16)


def draw_bias_weight(key, part):
    key_base = jax.random.fold_in(jax.random.fold_in(key, 23), 0)
    values = jnp.clip(jax.random.normal(key_base, (CZ, HEADS), jnp.float32), -4.0, 4.0) / jnp.sqrt(CZ * 1.0)
    return jnp.clip(values, -30.0, 30.0).astype(jnp.bfloat16)


def with_ends(entries, stream_key, low, top_value):
    longest = entries.shape.index(max(entries.shape))
    spots = []
    for shift in (0, 1):
        where = [jax.random.randint(jax.random.fold_in(stream_key, axis), (), 0, length) for axis, length in enumerate(entries.shape)]
        where[longest] = (where[longest] + shift) % entries.shape[longest]
        spots.append(tuple(where))
    return entries.at[spots[0]].set(low).at[spots[1]].set(top_value)


def steps_of(stream_key, extent, shards, low, largest):
    def one(dim, shards_of):
        heights = jax.random.uniform(jax.random.fold_in(jax.random.fold_in(stream_key, 6), dim), (shards_of,), jnp.float32, low / len(shards), largest / len(shards))
        return jnp.repeat(jnp.exp(heights), extent[dim] // shards_of).reshape((-1,) + (1,) * (len(extent) - dim - 1))

    level = one(*shards[0])
    for cut in shards[1:]:
        level = level * one(*cut)
    return level


def profile(number_of, total, reach, lean):
    portions = [(1 << 20) // math.isqrt(rank ** lean) + 1 for rank in range(2, number_of + 1)]
    spare, holding = total - reach - (number_of - 1), [1] * (number_of - 1)
    while spare > 0:
        candidates = [i for i in range(number_of - 1) if holding[i] < reach]
        whole, remaining = sum([portions[i] for i in candidates]), spare
        for i in candidates:
            more = min(reach - holding[i], max(1, remaining * portions[i] // whole), spare)
            holding[i] = holding[i] + more
            spare = spare - more
    return np.array([reach] + holding)


def uneven_parts(key, amount, total, most, skew):
    if amount == 2:
        one = jax.random.randint(key, (), max(1, total - most), min(most, total - 1) + 1)
        return jnp.stack([one, total - one])
    tallies = jnp.asarray(profile(amount, total, most, skew), jnp.int32)
    couples = (amount - 1) // 2
    donor, taker = tallies[1:1 + 2 * couples:2], tallies[2:2 + 2 * couples:2]
    room = jnp.minimum(donor - 1, most - taker)
    passed = jax.random.randint(jax.random.fold_in(key, 1), (couples,), 0, 1 << 20) % (room + 1)
    tallies = tallies.at[1:1 + 2 * couples:2].set(donor - passed).at[2:2 + 2 * couples:2].set(taker + passed)
    return tallies[jax.random.permutation(jax.random.fold_in(key, 2), amount)]


def bell_draw(stream_key, shape, width, limit, shards=(), held_as=jnp.bfloat16):
    values = width * jax.random.normal(stream_key, shape, jnp.float32)
    if shards:
        values = values * steps_of(stream_key, shape, shards, -0.22, 0.18)
    return jnp.clip(values, -limit, limit).astype(held_as)


def setup_inputs(seed: int = 0, part: int = 0) -> dict:
    keys = jax.random.split(jax.random.key(seed), 24)
    part_keys = jax.random.split(jax.random.fold_in(keys[23], part), 24)
    single = draw_single(jax.random.fold_in(jax.random.fold_in(keys[23], part), 71), part)
    pair = bell_draw(part_keys[1], (RES, RES, CZ), 1.0, 6.0, ((0, 4), (1, 4)))
    chain = jnp.searchsorted(jnp.cumsum(uneven_parts(part_keys[2], CHAINS, RES, RES // 4, 1)), jnp.arange(RES), side="right").astype(jnp.int32)
    live = with_ends((jax.random.randint(part_keys[3], (RES,), 0, 8) < 7).astype(jnp.int32), jax.random.fold_in(part_keys[3], 1), 0, 1)
    step_index = jax.random.randint(part_keys[4], (1,), 0, TSTEPS).astype(jnp.int32)
    time_scale = bell_draw(keys[5], (TFREQ, CS), TFREQ ** -0.5, 0.375, ((1, 4),))
    time_shift = bell_draw(keys[6], (TFREQ, CS), TFREQ ** -0.5, 0.375, ((1, 4),))
    w_query = bell_draw(keys[7], (CS, CS), CS ** -0.5, 0.21875, ((1, 4),))
    w_key = bell_draw(keys[8], (CS, CS), CS ** -0.5, 0.21875, ((1, 4),))
    w_value = bell_draw(keys[9], (CS, CS), CS ** -0.5, 0.21875, ((1, 4),))
    w_gate = bell_draw(keys[10], (CS, CS), CS ** -0.5, 0.21875, ((1, 4),))
    w_out = bell_draw(keys[11], (CS, CS), CS ** -0.5, 0.21875, ((1, 4),))
    pair_gain = jnp.clip(1.0 + 0.18 * jax.random.normal(keys[12], (CZ,), jnp.float32), 0.1, 1.9)
    bias_weight = draw_bias_weight(jax.random.fold_in(keys[23], 71), part)
    chain_bias = bell_draw(keys[14], (2, HEADS), 1.0, 4.0, (), jnp.float32)
    outer_gain = jnp.clip(1.0 + 0.18 * jax.random.normal(keys[15], (CS,), jnp.float32), 0.1, 1.9)
    w_left = bell_draw(keys[16], (CS, OPM), CS ** -0.5, 0.21875, ((0, 4),), jnp.float32)
    w_right = bell_draw(keys[17], (CS, OPM), CS ** -0.5, 0.21875, ((0, 4),), jnp.float32)
    w_outer = bell_draw(keys[18], (OPM, OPM, CZ), (OPM * OPM) ** -0.5, 0.1875)
    outer_bias = bell_draw(keys[19], (CZ,), 1.0, 4.0, (), jnp.float32)
    trans_gain = jnp.clip(1.0 + 0.18 * jax.random.normal(keys[20], (CZ,), jnp.float32), 0.1, 1.9)
    w_in = bell_draw(keys[21], (CZ, 2 * HID), CZ ** -0.5, 0.5)
    w_down = bell_draw(keys[22], (HID, CZ), HID ** -0.5, 0.25)
    return {"single": single, "pair": pair, "chain": chain, "live": live, "step_index": step_index, "time_scale": time_scale, "time_shift": time_shift, "w_query": w_query, "w_key": w_key, "w_value": w_value, "w_gate": w_gate, "w_out": w_out, "pair_gain": pair_gain, "bias_weight": bias_weight, "chain_bias": chain_bias, "outer_gain": outer_gain, "w_left": w_left, "w_right": w_right, "w_outer": w_outer, "outer_bias": outer_bias, "trans_gain": trans_gain, "w_in": w_in, "w_down": w_down}


EPSILON = 1e-05
MASKED = -1000000000.0

def channel_norm(values, gain):
    row_mean = lax.optimization_barrier(jnp.mean(values, axis=-1, keepdims=True))
    spread = lax.optimization_barrier(jnp.mean(values * values, axis=-1, keepdims=True)) - row_mean * row_mean
    return (values - row_mean) * lax.rsqrt(spread + EPSILON) * gain

def time_embed(step_index, count):
    halfway = count // 2
    ladder = jnp.arange(halfway).astype(jnp.float32)
    freqs = jnp.exp(-math.log(10000.0) * ladder / halfway)
    angles = step_index[0].astype(jnp.float32) * freqs
    return jnp.concatenate([jnp.sin(angles), jnp.cos(angles)])

def head_scores(query_rows, key_rows, bias_terms, head_count):
    query_heads = query_rows.reshape(query_rows.shape[0], head_count, -1)
    key_heads = key_rows.reshape(key_rows.shape[0], head_count, -1)
    raw = jnp.einsum('qhd,khd->hqk', query_heads.astype(jnp.float32), key_heads.astype(jnp.float32))
    return raw * query_heads.shape[2] ** (-0.5) + bias_terms

def transition(updated, gain, w_in, w_down):
    flat = updated.reshape(-1, updated.shape[-1])
    normed = channel_norm(flat, gain).astype(jnp.bfloat16)
    mixed = jnp.dot(normed, w_in, preferred_element_type=jnp.float32)
    halfway = w_down.shape[0]
    hidden = (jax.nn.silu(mixed[:, :halfway]) * mixed[:, halfway:]).astype(jnp.bfloat16)
    result = flat + jnp.dot(hidden, w_down, preferred_element_type=jnp.float32)
    return result.astype(jnp.bfloat16).reshape(updated.shape)

def reference(single, pair, chain, live, step_index, time_scale, time_shift, w_query, w_key, w_value, w_gate, w_out, pair_gain, bias_weight, chain_bias, outer_gain, w_left, w_right, w_outer, outer_bias, trans_gain, w_in, w_down):
    single_f = single.astype(jnp.float32)
    embedded = time_embed(step_index, TFREQ).astype(jnp.bfloat16)
    mod_scale = jnp.dot(embedded[None], time_scale, preferred_element_type=jnp.float32)[0]
    mod_shift = jnp.dot(embedded[None], time_shift, preferred_element_type=jnp.float32)[0]
    normed = (channel_norm(single_f, 1.0 + mod_scale) + mod_shift).astype(jnp.bfloat16)
    query_all = jnp.dot(normed, w_query, preferred_element_type=jnp.float32).astype(jnp.bfloat16)
    key_all = jnp.dot(normed, w_key, preferred_element_type=jnp.float32).astype(jnp.bfloat16)
    value_all = jnp.dot(normed, w_value, preferred_element_type=jnp.float32).astype(jnp.bfloat16)
    gate_all = jnp.dot(normed, w_gate, preferred_element_type=jnp.float32).astype(jnp.bfloat16)
    value_heads = value_all.reshape(RES, HEADS, HD).astype(jnp.float32)
    live_key = jnp.where(live == 1, 0.0, MASKED).astype(jnp.float32)
    blocks = jnp.arange(RES // RB).astype(jnp.int32)

    def attend(block_id):
        row_start = (block_id * RB).astype(jnp.int32)
        pair_rows = lax.dynamic_slice_in_dim(pair, row_start, RB, 0)
        pair_normed = channel_norm(pair_rows.astype(jnp.float32), pair_gain).astype(jnp.bfloat16)
        bias_terms = jnp.einsum('qkc,ch->hqk', pair_normed.astype(jnp.float32), bias_weight.astype(jnp.float32))
        chain_rows = lax.dynamic_slice_in_dim(chain, row_start, RB, 0)
        same_chain = chain_rows[:, None] == chain[None, :]
        chain_terms = jnp.where(same_chain[None], chain_bias[0][:, None, None], chain_bias[1][:, None, None])
        bias_terms = bias_terms + chain_terms + live_key[None, None, :]
        query_rows = lax.dynamic_slice_in_dim(query_all, row_start, RB, 0)
        scores = head_scores(query_rows, key_all, bias_terms, HEADS)
        row_top = lax.optimization_barrier(jnp.max(scores, axis=2))
        weights_exp = jnp.exp(scores - row_top[:, :, None])
        row_sum = lax.optimization_barrier(jnp.sum(weights_exp, axis=2))
        attended = jnp.einsum('hqk,khd->qhd', weights_exp, value_heads, precision=lax.Precision.HIGHEST)
        attended = (attended / row_sum.T[:, :, None]).reshape(RB, CS)
        gate_rows = lax.dynamic_slice_in_dim(gate_all, row_start, RB, 0)
        return (jax.nn.sigmoid(gate_rows.astype(jnp.float32)) * attended).astype(jnp.bfloat16)
    gated = lax.map(attend, blocks).reshape(RES, CS)
    single_out = (single_f + jnp.dot(gated, w_out, preferred_element_type=jnp.float32)).astype(jnp.bfloat16)
    outer_normed = channel_norm(single_out.astype(jnp.float32), outer_gain)
    left = jnp.dot(outer_normed, w_left, precision=lax.Precision.HIGHEST).astype(jnp.bfloat16)
    right = jnp.dot(outer_normed, w_right, precision=lax.Precision.HIGHEST).astype(jnp.bfloat16)
    left_mix = jnp.einsum('ip,pqc->iqc', left.astype(jnp.float32), w_outer.astype(jnp.float32), precision=lax.Precision.HIGHEST)
    right_f = right.astype(jnp.float32)
    live_f = live.astype(jnp.float32)

    def update(block_id):
        row_start = (block_id * RB).astype(jnp.int32)
        pair_rows = lax.dynamic_slice_in_dim(pair, row_start, RB, 0)
        left_rows = lax.dynamic_slice_in_dim(left_mix, row_start, RB, 0)
        live_rows = lax.dynamic_slice_in_dim(live_f, row_start, RB, 0)
        outer = jnp.einsum('iqc,jq->ijc', left_rows, right_f, precision=lax.Precision.HIGHEST) + outer_bias
        outer = outer * (live_rows[:, None] * live_f[None, :])[:, :, None]
        updated = pair_rows.astype(jnp.float32) + outer
        return transition(updated, trans_gain, w_in, w_down)
    pair_out = lax.map(update, blocks).reshape(RES, RES, CZ)
    return (single_out, pair_out)
```

```python
import functools
import math

import jax
import jax.numpy as jnp
from jax import lax
from jax.experimental import pallas as pl
from jax.experimental.pallas import tpu as pltpu
from jax.sharding import PartitionSpec as P

EPSILON = 1e-05
MASKED = -1000000000.0


def broadcast(array, axis, root):
    mine = lax.axis_index(axis) == root
    return lax.psum(jnp.where(mine, array, jnp.zeros_like(array)), axis)


def channel_norm(values, gain):
    row_mean = jnp.mean(values, axis=-1, keepdims=True)
    spread = jnp.mean(values * values, axis=-1, keepdims=True) - row_mean * row_mean
    return (values - row_mean) * lax.rsqrt(spread + EPSILON) * gain


def time_embed(step_index, count):
    halfway = count // 2
    ladder = jnp.arange(halfway).astype(jnp.float32)
    freqs = jnp.exp(-math.log(10000.0) * ladder / halfway)
    angles = step_index[0].astype(jnp.float32) * freqs
    return jnp.concatenate([jnp.sin(angles), jnp.cos(angles)])


def head_scores(query_rows, key_rows, bias_terms, head_count):
    query_heads = query_rows.reshape(query_rows.shape[0], head_count, -1)
    key_heads = key_rows.reshape(key_rows.shape[0], head_count, -1)
    raw = jnp.einsum("qhd,khd->hqk", query_heads, key_heads, preferred_element_type=jnp.float32)
    return raw * query_heads.shape[2] ** (-0.5) + bias_terms


def weighted_values(weights_exp, value_rows, head_count):
    value_heads = value_rows.reshape(value_rows.shape[0], head_count, -1).astype(jnp.float32)
    summed = jnp.einsum("hqk,khd->qhd", weights_exp, value_heads, precision=lax.Precision.HIGHEST)
    return summed.reshape(summed.shape[0], -1)


def divide_heads(summed, totals):
    row_count = summed.shape[0]
    head_count = totals.shape[0]
    return (summed.reshape(row_count, head_count, -1) / totals.T[:, :, None]).reshape(row_count, -1)


def transition(flat, gain, w_in, w_down):
    normed = channel_norm(flat, gain).astype(jnp.bfloat16)
    mixed = jnp.dot(normed, w_in, preferred_element_type=jnp.float32)
    halfway = w_down.shape[0]
    hidden = (jax.nn.silu(mixed[:, :halfway]) * mixed[:, halfway:]).astype(jnp.bfloat16)
    return (flat + jnp.dot(hidden, w_down, preferred_element_type=jnp.float32)).astype(jnp.bfloat16)


def body(
    single,
    pair,
    chain,
    live,
    step_index,
    time_scale,
    time_shift,
    w_query,
    w_key,
    w_value,
    w_gate,
    w_out,
    pair_gain,
    bias_weight,
    chain_bias,
    outer_gain,
    w_left,
    w_right,
    w_outer,
    outer_bias,
    trans_gain,
    w_in,
    w_down,
):
    block_rows = single.shape[0]
    model_width = w_query.shape[0]
    head_count = chain_bias.shape[1]
    row_place = lax.axis_index("row")
    col_place = lax.axis_index("col")
    query_start = row_place * block_rows
    key_start = col_place * block_rows
    chain_query = lax.dynamic_slice_in_dim(chain, query_start, block_rows, 0)
    chain_key = lax.dynamic_slice_in_dim(chain, key_start, block_rows, 0)
    live_query = lax.dynamic_slice_in_dim(live, query_start, block_rows, 0).astype(jnp.float32)
    live_keys = lax.dynamic_slice_in_dim(live, key_start, block_rows, 0)
    single_f = single.astype(jnp.float32)
    totals = lax.psum((jnp.sum(single_f, axis=1), jnp.sum(single_f * single_f, axis=1)), "col")
    row_mean = totals[0] / model_width
    inv_std = lax.rsqrt(totals[1] / model_width - row_mean * row_mean + EPSILON)
    embedded = time_embed(step_index, time_scale.shape[0]).astype(jnp.bfloat16)
    mod_scale = jnp.dot(embedded[None], time_scale, preferred_element_type=jnp.float32)[0]
    mod_shift = jnp.dot(embedded[None], time_shift, preferred_element_type=jnp.float32)[0]
    normed = (
        (single_f - row_mean[:, None]) * inv_std[:, None] * (1.0 + mod_scale) + mod_shift
    ).astype(jnp.bfloat16)
    normed_full = lax.all_gather(normed, "col", axis=1, tiled=True)
    query_part = jnp.dot(normed_full, w_query, preferred_element_type=jnp.float32).astype(
        jnp.bfloat16
    )
    key_part = jnp.dot(normed_full, w_key, preferred_element_type=jnp.float32).astype(jnp.bfloat16)
    value_part = jnp.dot(normed_full, w_value, preferred_element_type=jnp.float32).astype(
        jnp.bfloat16
    )
    gate_part = jnp.dot(normed_full, w_gate, preferred_element_type=jnp.float32).astype(
        jnp.bfloat16
    )
    query_full, key_full, value_full, gate_full = (
        lax.all_gather(query_part, "col", axis=1, tiled=True),
        lax.all_gather(key_part, "col", axis=1, tiled=True),
        lax.all_gather(value_part, "col", axis=1, tiled=True),
        lax.all_gather(gate_part, "col", axis=1, tiled=True),
    )
    key_cols, value_cols = (
        broadcast(key_full, "row", col_place),
        broadcast(value_full, "row", col_place),
    )
    pair_normed = channel_norm(pair.astype(jnp.float32), pair_gain).astype(jnp.bfloat16)
    bias_terms = jnp.einsum(
        "qkc,ch->hqk", pair_normed, bias_weight, preferred_element_type=jnp.float32
    )
    same_chain = chain_query[:, None] == chain_key[None, :]
    chain_terms = jnp.where(
        same_chain[None], chain_bias[0][:, None, None], chain_bias[1][:, None, None]
    )
    live_terms = jnp.where(live_keys == 1, 0.0, MASKED).astype(jnp.float32)
    bias_terms = bias_terms + chain_terms + live_terms[None, None, :]
    scores = head_scores(query_full, key_cols, bias_terms, head_count)
    row_top = lax.pmax(jnp.max(scores, axis=2), "col")
    weights_exp = jnp.exp(scores - row_top[:, :, None])
    row_sum, summed = lax.psum(
        (jnp.sum(weights_exp, axis=2), weighted_values(weights_exp, value_cols, head_count)), "col"
    )
    attended = divide_heads(summed, row_sum)
    gated = (jax.nn.sigmoid(gate_full.astype(jnp.float32)) * attended).astype(jnp.bfloat16)
    single_out = (single_f + jnp.dot(gated, w_out, preferred_element_type=jnp.float32)).astype(
        jnp.bfloat16
    )
    updated_single = single_out.astype(jnp.float32)
    gained = updated_single * outer_gain
    joint = lax.psum(
        (
            jnp.sum(updated_single, axis=1),
            jnp.sum(updated_single * updated_single, axis=1),
            jnp.dot(gained, w_left, precision=lax.Precision.HIGHEST),
            jnp.dot(gained, w_right, precision=lax.Precision.HIGHEST),
            jnp.dot(outer_gain[None], w_left, precision=lax.Precision.HIGHEST)[0],
            jnp.dot(outer_gain[None], w_right, precision=lax.Precision.HIGHEST)[0],
        ),
        "col",
    )
    out_mean = joint[0] / model_width
    out_inv = lax.rsqrt(joint[1] / model_width - out_mean * out_mean + EPSILON)
    left_full = out_inv[:, None] * (joint[2] - out_mean[:, None] * joint[4][None, :])
    right_full = out_inv[:, None] * (joint[3] - out_mean[:, None] * joint[5][None, :])
    left_rows = left_full.astype(jnp.bfloat16)
    right_rows = right_full.astype(jnp.bfloat16)
    right_cols = broadcast(right_rows, "row", col_place)
    left_mix = jnp.einsum("ip,pqc->iqc", left_rows, w_outer, preferred_element_type=jnp.float32)
    outer = (
        jnp.einsum(
            "iqc,jq->ijc", left_mix, right_cols.astype(jnp.float32), precision=lax.Precision.HIGHEST
        )
        + outer_bias
    )
    outer = outer * (live_query[:, None] * live_keys.astype(jnp.float32)[None, :])[:, :, None]
    updated = pair.astype(jnp.float32) + outer
    flat = updated.reshape(-1, updated.shape[-1])
    total_rows = flat.shape[0]
    piece_rows = math.gcd(total_rows, 1024)
    pieces = flat.reshape(total_rows // piece_rows, piece_rows, flat.shape[1])
    pair_out = lax.map(lambda piece: transition(piece, trans_gain, w_in, w_down), pieces).reshape(
        pair.shape
    )
    return (single_out, pair_out)


MESH_ID = pl.DeviceIdType.MESH


def attention_kernel(
    row_count,
    col_count,
    head_size,
    single_ref,
    embedded_ref,
    scale_ref,
    shift_ref,
    query_w_ref,
    key_w_ref,
    value_w_ref,
    gate_w_ref,
    out_w_ref,
    bias_ref,
    gain_ref,
    factors_ref,
    single_out_ref,
    left_ref,
    right_ref,
    singles,
    mods,
    biases,
    keys_values,
    gates,
    left_parts,
    right_parts,
    col_send,
    col_recv,
    row_send,
    row_recv,
    right_send,
    right_recv,
):
    row_place = lax.axis_index("row")
    col_place = lax.axis_index("col")
    rows, width = single_ref.shape
    model_width = query_w_ref.shape[0]
    factor = left_ref.shape[1]
    head_count = width // head_size

    def col_peer(step):
        return {"col": lax.rem(col_place + step, col_count)}

    def row_peer(step):
        return {"row": lax.rem(row_place + step, row_count)}

    def copy(source, target, send, recv, device):
        return pltpu.make_async_remote_copy(
            src_ref=source,
            dst_ref=target,
            send_sem=send,
            recv_sem=recv,
            device_id=device,
            device_id_type=MESH_ID,
        )

    barrier = pltpu.get_barrier_semaphore()
    for row_step in range(row_count):
        for col_step in range(col_count):
            if row_step or col_step:
                pl.semaphore_signal(
                    barrier,
                    inc=1,
                    device_id=row_peer(row_step) | col_peer(col_step),
                    device_id_type=MESH_ID,
                )
    embedded = embedded_ref[...]
    mod_scale = jnp.dot(embedded, scale_ref[...], preferred_element_type=jnp.float32)
    mod_shift = jnp.dot(embedded, shift_ref[...], preferred_element_type=jnp.float32)
    mods[col_place, 0] = mod_scale[:8]
    mods[col_place, 1] = mod_shift[:8]
    singles[col_place] = single_ref[...]
    pl.semaphore_wait(barrier, row_count * col_count - 1)

    first = []
    bias_copies = []
    for step in range(1, col_count):
        peer = col_peer(step)
        first.append(
            copy(
                single_ref,
                singles.at[col_place],
                col_send.at[0, step],
                col_recv.at[0, step],
                peer,
            )
        )
        first.append(
            copy(
                mods.at[col_place],
                mods.at[col_place],
                col_send.at[1, step],
                col_recv.at[1, step],
                peer,
            )
        )
        bias_copies.append(
            copy(
                bias_ref.at[lax.rem(col_place + step, col_count)],
                biases.at[col_place],
                col_send.at[2, step],
                col_recv.at[2, step],
                peer,
            )
        )
    for each in first:
        each.start()
    for each in bias_copies:
        each.start()
    biases[col_place] = bias_ref[col_place]
    for each in first:
        each.wait()

    total = jnp.zeros((rows, 1), jnp.float32)
    squares = jnp.zeros((rows, 1), jnp.float32)
    for block in range(col_count):
        piece = singles[block].astype(jnp.float32)
        total = total + jnp.sum(piece, axis=1, keepdims=True)
        squares = squares + jnp.sum(piece * piece, axis=1, keepdims=True)
    mean = total / model_width
    inv = lax.rsqrt(squares / model_width - mean * mean + EPSILON)
    query = jnp.zeros((rows, width), jnp.float32)
    key = jnp.zeros((rows, width), jnp.float32)
    value = jnp.zeros((rows, width), jnp.float32)
    gate = jnp.zeros((rows, width), jnp.float32)
    for block in range(col_count):
        piece = singles[block].astype(jnp.float32)
        normed = (piece - mean) * inv * (1.0 + mods[block, 0, 0:1]) + mods[block, 1, 0:1]
        normed = normed.astype(jnp.bfloat16)
        span = pl.ds(block * width, width)
        key += jnp.dot(normed, key_w_ref[span, :], preferred_element_type=jnp.float32)
        value += jnp.dot(normed, value_w_ref[span, :], preferred_element_type=jnp.float32)
        query += jnp.dot(normed, query_w_ref[span, :], preferred_element_type=jnp.float32)
        gate += jnp.dot(normed, gate_w_ref[span, :], preferred_element_type=jnp.float32)
    keys_values[row_place, 0] = key.astype(jnp.bfloat16)
    keys_values[row_place, 1] = value.astype(jnp.bfloat16)
    second = [
        copy(
            keys_values.at[row_place],
            keys_values.at[row_place],
            row_send.at[step],
            row_recv.at[step],
            row_peer(step),
        )
        for step in range(1, row_count)
    ]
    for each in second:
        each.start()
    opened = jax.nn.sigmoid(gate.astype(jnp.bfloat16).astype(jnp.float32))
    query = query.astype(jnp.bfloat16)
    lane = lax.broadcasted_iota(jnp.int32, (rows, width), 1)
    masks = [
        (lane >= head * head_size) & (lane < (head + 1) * head_size) for head in range(head_count)
    ]
    query_heads = jnp.concatenate(
        [jnp.where(mask, query, jnp.zeros_like(query)) for mask in masks], axis=0
    )
    for each in bias_copies:
        each.wait()
    for each in second:
        each.wait()
    scores = [
        lax.dot_general(
            query_heads,
            keys_values[block, 0],
            (((1,), (1,)), ((), ())),
            preferred_element_type=jnp.float32,
        )
        * head_size ** (-0.5)
        + biases[block]
        for block in range(row_count)
    ]
    top = functools.reduce(jnp.maximum, [jnp.max(s, axis=1, keepdims=True) for s in scores])
    weights = [jnp.exp(s - top) for s in scores]
    weight_sum = sum(jnp.sum(w, axis=1, keepdims=True) for w in weights)
    summed = sum(
        jnp.dot(
            weights[block].astype(jnp.bfloat16),
            keys_values[block, 1],
            preferred_element_type=jnp.float32,
        )
        for block in range(row_count)
    )
    summed = summed / weight_sum
    attended = sum(
        jnp.where(masks[head], summed[head * rows : (head + 1) * rows], 0.0)
        for head in range(head_count)
    )
    gates[col_place] = (opened * attended).astype(jnp.bfloat16)
    third = [
        copy(
            gates.at[col_place],
            gates.at[col_place],
            col_send.at[3, step],
            col_recv.at[3, step],
            col_peer(step),
        )
        for step in range(1, col_count)
    ]
    for each in third:
        each.start()
    for each in third:
        each.wait()
    mixed = single_ref[...].astype(jnp.float32)
    for block in range(col_count):
        mixed += jnp.dot(
            gates[block],
            out_w_ref[pl.ds(block * width, width), :],
            preferred_element_type=jnp.float32,
        )
    single_out = mixed.astype(jnp.bfloat16)
    single_out_ref[...] = single_out
    updated = single_out.astype(jnp.float32)
    gain = gain_ref[...]
    stacked = jnp.concatenate([updated * gain, jnp.broadcast_to(gain, (8, width))], axis=0)
    products = jnp.dot(
        stacked,
        factors_ref[...],
        precision=lax.Precision.HIGHEST,
        preferred_element_type=jnp.float32,
    )
    place = lax.broadcasted_iota(jnp.int32, (rows, products.shape[1]), 1)
    left_parts[col_place, pl.ds(0, rows), :] = jnp.where(
        place == 2 * factor,
        jnp.sum(updated, axis=1, keepdims=True),
        jnp.where(
            place == 2 * factor + 1,
            jnp.sum(updated * updated, axis=1, keepdims=True),
            products[:rows],
        ),
    )
    left_parts[col_place, pl.ds(rows, 8), :] = products[rows:]
    fourth = [
        copy(
            left_parts.at[col_place],
            left_parts.at[col_place],
            col_send.at[4, step],
            col_recv.at[4, step],
            col_peer(step),
        )
        for step in range(1, col_count)
    ]
    right_copies = [
        copy(
            left_parts.at[col_place],
            right_parts.at[col_place],
            right_send.at[step],
            right_recv.at[col_place],
            row_peer(step) | {"col": row_place},
        )
        for step in range(row_count)
    ]
    diagonal = row_place == col_place
    for each in fourth:
        each.start()
    for step in range(1, row_count):
        right_copies[step].start()

    @pl.when(jnp.logical_not(diagonal))
    def _():
        right_copies[0].start()

    @pl.when(diagonal)
    def _():
        right_parts[col_place] = left_parts[col_place]

    for each in fourth:
        each.wait()

    def finish(parts):
        joint = parts[0]
        for block in range(1, col_count):
            joint = joint + parts[block]
        body_rows = joint[:rows]
        out_mean = body_rows[:, 2 * factor : 2 * factor + 1] / model_width
        out_square = body_rows[:, 2 * factor + 1 : 2 * factor + 2] / model_width
        out_inv = lax.rsqrt(out_square - out_mean * out_mean + EPSILON)
        return out_inv * (body_rows - out_mean * joint[rows : rows + 1])

    left_ref[...] = finish(left_parts)[:, :factor].astype(jnp.bfloat16)
    for block in range(col_count):

        @pl.when(jnp.logical_not(diagonal & (col_place == block)))
        def _():
            copy(
                left_parts.at[block],
                right_parts.at[block],
                right_send.at[0],
                right_recv.at[block],
                row_peer(0),
            ).wait_recv()

    right_ref[...] = finish(right_parts)[:, factor : 2 * factor].astype(jnp.bfloat16)
    for step in range(1, row_count):
        right_copies[step].wait_send()

    @pl.when(jnp.logical_not(diagonal))
    def _():
        right_copies[0].wait_send()


def pair_kernel(
    live_ref,
    pair_ref,
    mix_ref,
    right_ref,
    live_keys_ref,
    outer_bias_ref,
    gain_ref,
    w_in_ref,
    w_down_ref,
    out_ref,
    flat_ref,
):
    block_rows, key_rows, channels = pair_ref.shape
    start = pl.program_id(0) * block_rows
    right = right_ref[...]
    right_twice = jnp.concatenate([right, right], axis=1)
    live_keys = live_keys_ref[...]
    outer_bias = outer_bias_ref[...]
    for place in range(block_rows):
        mix = mix_ref[place]
        high = mix.astype(jnp.bfloat16)
        low = (mix - high.astype(jnp.float32)).astype(jnp.bfloat16)
        outer = jnp.dot(
            right_twice,
            jnp.concatenate([high, low], axis=0),
            preferred_element_type=jnp.float32,
        )
        outer = (outer + outer_bias) * (live_keys * live_ref[start + place])
        flat_ref[pl.ds(place * key_rows, key_rows), :] = pair_ref[place].astype(jnp.float32) + outer
    flat = flat_ref[...]
    normed = channel_norm(flat, gain_ref[...]).astype(jnp.bfloat16)
    hidden_width = w_down_ref.shape[0]
    chunk = math.gcd(hidden_width, 256)
    result = flat
    for first in range(0, hidden_width, chunk):
        gate = jnp.dot(normed, w_in_ref[:, first : first + chunk], preferred_element_type=jnp.float32)
        up = jnp.dot(
            normed,
            w_in_ref[:, hidden_width + first : hidden_width + first + chunk],
            preferred_element_type=jnp.float32,
        )
        half = gate * 0.5
        hidden = ((half + half * jnp.tanh(half)) * up).astype(jnp.bfloat16)
        result = result + jnp.dot(
            hidden, w_down_ref[first : first + chunk, :], preferred_element_type=jnp.float32
        )
    out_ref[...] = result.astype(jnp.bfloat16).reshape(out_ref.shape)


def fast_body(
    row_count,
    col_count,
    single,
    pair,
    chain,
    live,
    step_index,
    time_scale,
    time_shift,
    w_query,
    w_key,
    w_value,
    w_gate,
    w_out,
    pair_gain,
    bias_weight,
    chain_bias,
    outer_gain,
    w_left,
    w_right,
    w_outer,
    outer_bias,
    trans_gain,
    w_in,
    w_down,
):
    rows, width = single.shape
    model_width = w_query.shape[0]
    head_count = chain_bias.shape[1]
    head_size = model_width // head_count
    local_heads = head_count // col_count
    factor = w_left.shape[1]
    channels = pair.shape[2]
    query_start = lax.axis_index("row") * rows
    key_start = lax.axis_index("col") * rows
    chain_query = lax.dynamic_slice_in_dim(chain, query_start, rows, 0)
    chain_key = lax.dynamic_slice_in_dim(chain, key_start, rows, 0)
    live_query = lax.dynamic_slice_in_dim(live, query_start, rows, 0).astype(jnp.float32)
    live_keys = lax.dynamic_slice_in_dim(live, key_start, rows, 0)
    embedded = time_embed(step_index, time_scale.shape[0]).astype(jnp.bfloat16)
    embedded = jnp.broadcast_to(embedded[None], (16, embedded.shape[0]))
    pair_normed = channel_norm(pair.astype(jnp.float32), pair_gain).astype(jnp.bfloat16)
    bias_terms = jnp.einsum(
        "qkc,ch->hqk", pair_normed, bias_weight, preferred_element_type=jnp.float32
    )
    same_chain = chain_query[:, None] == chain_key[None, :]
    chain_terms = jnp.where(
        same_chain[None], chain_bias[0][:, None, None], chain_bias[1][:, None, None]
    )
    live_terms = jnp.where(live_keys == 1, 0.0, MASKED).astype(jnp.float32)
    bias_terms = bias_terms + chain_terms + live_terms[None, None, :]
    bias_terms = bias_terms.reshape(col_count, local_heads * rows, rows)
    lanes = 128 * pl.cdiv(2 * factor + 2, 128)
    factors = jnp.concatenate(
        [w_left, w_right, jnp.zeros((width, lanes - 2 * factor), jnp.float32)], axis=1
    )
    vmem = pl.BlockSpec(memory_space=pltpu.VMEM)
    bf16, f32 = jnp.bfloat16, jnp.float32
    single_out, left, right = pl.pallas_call(
        functools.partial(attention_kernel, row_count, col_count, head_size),
        out_shape=(
            jax.ShapeDtypeStruct((rows, width), bf16),
            jax.ShapeDtypeStruct((rows, factor), bf16),
            jax.ShapeDtypeStruct((rows, factor), bf16),
        ),
        in_specs=[vmem] * 12,
        out_specs=(vmem, vmem, vmem),
        scratch_shapes=[
            pltpu.VMEM((col_count, rows, width), bf16),
            pltpu.VMEM((col_count, 2, 8, width), f32),
            pltpu.VMEM((col_count, local_heads * rows, rows), f32),
            pltpu.VMEM((row_count, 2, rows, width), bf16),
            pltpu.VMEM((col_count, rows, width), bf16),
            pltpu.VMEM((col_count, rows + 8, lanes), f32),
            pltpu.VMEM((col_count, rows + 8, lanes), f32),
            pltpu.SemaphoreType.DMA((5, col_count)),
            pltpu.SemaphoreType.DMA((5, col_count)),
            pltpu.SemaphoreType.DMA((row_count,)),
            pltpu.SemaphoreType.DMA((row_count,)),
            pltpu.SemaphoreType.DMA((row_count,)),
            pltpu.SemaphoreType.DMA((col_count,)),
        ],
        compiler_params=pltpu.CompilerParams(collective_id=0, has_side_effects=True),
        name="attention",
    )(
        single,
        embedded,
        time_scale,
        time_shift,
        w_query,
        w_key,
        w_value,
        w_gate,
        w_out,
        bias_terms,
        outer_gain[None],
        factors,
    )
    left_mix = jnp.einsum("ip,pqc->iqc", left, w_outer, preferred_element_type=jnp.float32)
    live_lanes = jnp.broadcast_to(live_keys.astype(jnp.float32)[:, None], (rows, channels))
    block = math.gcd(rows, 8)
    hidden = w_down.shape[0]
    pair_out = pl.pallas_call(
        pair_kernel,
        grid=(rows // block,),
        out_shape=jax.ShapeDtypeStruct(pair.shape, bf16),
        in_specs=[
            pl.BlockSpec(memory_space=pltpu.SMEM),
            pl.BlockSpec((block, rows, channels), lambda i: (i, 0, 0)),
            pl.BlockSpec((block, factor, channels), lambda i: (i, 0, 0)),
            pl.BlockSpec((rows, factor), lambda i: (0, 0)),
            pl.BlockSpec((rows, channels), lambda i: (0, 0)),
            pl.BlockSpec((1, channels), lambda i: (0, 0)),
            pl.BlockSpec((1, channels), lambda i: (0, 0)),
            pl.BlockSpec((channels, 2 * hidden), lambda i: (0, 0)),
            pl.BlockSpec((hidden, channels), lambda i: (0, 0)),
        ],
        out_specs=pl.BlockSpec((block, rows, channels), lambda i: (i, 0, 0)),
        scratch_shapes=[pltpu.VMEM((block * rows, channels), f32)],
        name="transition",
    )(
        live_query,
        pair,
        left_mix,
        right,
        live_lanes,
        outer_bias[None],
        trans_gain[None],
        w_in,
        w_down,
    )
    return (single_out, pair_out)


def solution(mesh):
    in_specs = (
        P(("groups", "row"), "col"),
        P(("groups", "row"), "col", None),
        P("groups"),
        P("groups"),
        P("groups"),
        P(None, "col"),
        P(None, "col"),
        P(None, "col"),
        P(None, "col"),
        P(None, "col"),
        P(None, "col"),
        P(None, "col"),
        P(),
        P(),
        P(),
        P("col"),
        P("col", None),
        P("col", None),
        P(),
        P(),
        P(),
        P(),
        P(),
    )
    out_specs = (P(("groups", "row"), "col"), P(("groups", "row"), "col", None))
    row_count, col_count = mesh.shape["row"], mesh.shape["col"]

    def chosen(*args):
        head_count = args[14].shape[1]
        if row_count == col_count and head_count % col_count == 0:
            return fast_body(row_count, col_count, *args)
        return body(*args)

    return jax.shard_map(chosen, mesh=mesh, in_specs=in_specs, out_specs=out_specs, check_vma=False)
```

```python
import functools
import math

import jax
import jax.numpy as jnp
from jax import lax
from jax.experimental import pallas as pl
from jax.experimental.pallas import tpu as pltpu
from jax.sharding import PartitionSpec as P

EPSILON = 1e-05
MASKED = -1000000000.0


def broadcast(array, axis, root):
    mine = lax.axis_index(axis) == root
    return lax.psum(jnp.where(mine, array, jnp.zeros_like(array)), axis)


def channel_norm(values, gain):
    row_mean = jnp.mean(values, axis=-1, keepdims=True)
    spread = jnp.mean(values * values, axis=-1, keepdims=True) - row_mean * row_mean
    return (values - row_mean) * lax.rsqrt(spread + EPSILON) * gain


def time_embed(step_index, count):
    halfway = count // 2
    ladder = jnp.arange(halfway).astype(jnp.float32)
    freqs = jnp.exp(-math.log(10000.0) * ladder / halfway)
    angles = step_index[0].astype(jnp.float32) * freqs
    return jnp.concatenate([jnp.sin(angles), jnp.cos(angles)])


def head_scores(query_rows, key_rows, bias_terms, head_count):
    query_heads = query_rows.reshape(query_rows.shape[0], head_count, -1)
    key_heads = key_rows.reshape(key_rows.shape[0], head_count, -1)
    raw = jnp.einsum("qhd,khd->hqk", query_heads, key_heads, preferred_element_type=jnp.float32)
    return raw * query_heads.shape[2] ** (-0.5) + bias_terms


def weighted_values(weights_exp, value_rows, head_count):
    value_heads = value_rows.reshape(value_rows.shape[0], head_count, -1).astype(jnp.float32)
    summed = jnp.einsum("hqk,khd->qhd", weights_exp, value_heads, precision=lax.Precision.HIGHEST)
    return summed.reshape(summed.shape[0], -1)


def divide_heads(summed, totals):
    row_count = summed.shape[0]
    head_count = totals.shape[0]
    return (summed.reshape(row_count, head_count, -1) / totals.T[:, :, None]).reshape(row_count, -1)


def transition(flat, gain, w_in, w_down):
    normed = channel_norm(flat, gain).astype(jnp.bfloat16)
    mixed = jnp.dot(normed, w_in, preferred_element_type=jnp.float32)
    halfway = w_down.shape[0]
    hidden = (jax.nn.silu(mixed[:, :halfway]) * mixed[:, halfway:]).astype(jnp.bfloat16)
    return (flat + jnp.dot(hidden, w_down, preferred_element_type=jnp.float32)).astype(jnp.bfloat16)


def body(
    single,
    pair,
    chain,
    live,
    step_index,
    time_scale,
    time_shift,
    w_query,
    w_key,
    w_value,
    w_gate,
    w_out,
    pair_gain,
    bias_weight,
    chain_bias,
    outer_gain,
    w_left,
    w_right,
    w_outer,
    outer_bias,
    trans_gain,
    w_in,
    w_down,
):
    block_rows = single.shape[0]
    model_width = w_query.shape[0]
    head_count = chain_bias.shape[1]
    row_place = lax.axis_index("row")
    col_place = lax.axis_index("col")
    query_start = row_place * block_rows
    key_start = col_place * block_rows
    chain_query = lax.dynamic_slice_in_dim(chain, query_start, block_rows, 0)
    chain_key = lax.dynamic_slice_in_dim(chain, key_start, block_rows, 0)
    live_query = lax.dynamic_slice_in_dim(live, query_start, block_rows, 0).astype(jnp.float32)
    live_keys = lax.dynamic_slice_in_dim(live, key_start, block_rows, 0)
    single_f = single.astype(jnp.float32)
    totals = lax.psum((jnp.sum(single_f, axis=1), jnp.sum(single_f * single_f, axis=1)), "col")
    row_mean = totals[0] / model_width
    inv_std = lax.rsqrt(totals[1] / model_width - row_mean * row_mean + EPSILON)
    embedded = time_embed(step_index, time_scale.shape[0]).astype(jnp.bfloat16)
    mod_scale = jnp.dot(embedded[None], time_scale, preferred_element_type=jnp.float32)[0]
    mod_shift = jnp.dot(embedded[None], time_shift, preferred_element_type=jnp.float32)[0]
    normed = (
        (single_f - row_mean[:, None]) * inv_std[:, None] * (1.0 + mod_scale) + mod_shift
    ).astype(jnp.bfloat16)
    normed_full = lax.all_gather(normed, "col", axis=1, tiled=True)
    query_part = jnp.dot(normed_full, w_query, preferred_element_type=jnp.float32).astype(
        jnp.bfloat16
    )
    key_part = jnp.dot(normed_full, w_key, preferred_element_type=jnp.float32).astype(jnp.bfloat16)
    value_part = jnp.dot(normed_full, w_value, preferred_element_type=jnp.float32).astype(
        jnp.bfloat16
    )
    gate_part = jnp.dot(normed_full, w_gate, preferred_element_type=jnp.float32).astype(
        jnp.bfloat16
    )
    query_full, key_full, value_full, gate_full = (
        lax.all_gather(query_part, "col", axis=1, tiled=True),
        lax.all_gather(key_part, "col", axis=1, tiled=True),
        lax.all_gather(value_part, "col", axis=1, tiled=True),
        lax.all_gather(gate_part, "col", axis=1, tiled=True),
    )
    key_cols, value_cols = (
        broadcast(key_full, "row", col_place),
        broadcast(value_full, "row", col_place),
    )
    pair_normed = channel_norm(pair.astype(jnp.float32), pair_gain).astype(jnp.bfloat16)
    bias_terms = jnp.einsum(
        "qkc,ch->hqk", pair_normed, bias_weight, preferred_element_type=jnp.float32
    )
    same_chain = chain_query[:, None] == chain_key[None, :]
    chain_terms = jnp.where(
        same_chain[None], chain_bias[0][:, None, None], chain_bias[1][:, None, None]
    )
    live_terms = jnp.where(live_keys == 1, 0.0, MASKED).astype(jnp.float32)
    bias_terms = bias_terms + chain_terms + live_terms[None, None, :]
    scores = head_scores(query_full, key_cols, bias_terms, head_count)
    row_top = lax.pmax(jnp.max(scores, axis=2), "col")
    weights_exp = jnp.exp(scores - row_top[:, :, None])
    row_sum, summed = lax.psum(
        (jnp.sum(weights_exp, axis=2), weighted_values(weights_exp, value_cols, head_count)), "col"
    )
    attended = divide_heads(summed, row_sum)
    gated = (jax.nn.sigmoid(gate_full.astype(jnp.float32)) * attended).astype(jnp.bfloat16)
    single_out = (single_f + jnp.dot(gated, w_out, preferred_element_type=jnp.float32)).astype(
        jnp.bfloat16
    )
    updated_single = single_out.astype(jnp.float32)
    gained = updated_single * outer_gain
    joint = lax.psum(
        (
            jnp.sum(updated_single, axis=1),
            jnp.sum(updated_single * updated_single, axis=1),
            jnp.dot(gained, w_left, precision=lax.Precision.HIGHEST),
            jnp.dot(gained, w_right, precision=lax.Precision.HIGHEST),
            jnp.dot(outer_gain[None], w_left, precision=lax.Precision.HIGHEST)[0],
            jnp.dot(outer_gain[None], w_right, precision=lax.Precision.HIGHEST)[0],
        ),
        "col",
    )
    out_mean = joint[0] / model_width
    out_inv = lax.rsqrt(joint[1] / model_width - out_mean * out_mean + EPSILON)
    left_full = out_inv[:, None] * (joint[2] - out_mean[:, None] * joint[4][None, :])
    right_full = out_inv[:, None] * (joint[3] - out_mean[:, None] * joint[5][None, :])
    left_rows = left_full.astype(jnp.bfloat16)
    right_rows = right_full.astype(jnp.bfloat16)
    right_cols = broadcast(right_rows, "row", col_place)
    left_mix = jnp.einsum("ip,pqc->iqc", left_rows, w_outer, preferred_element_type=jnp.float32)
    outer = (
        jnp.einsum(
            "iqc,jq->ijc", left_mix, right_cols.astype(jnp.float32), precision=lax.Precision.HIGHEST
        )
        + outer_bias
    )
    outer = outer * (live_query[:, None] * live_keys.astype(jnp.float32)[None, :])[:, :, None]
    updated = pair.astype(jnp.float32) + outer
    flat = updated.reshape(-1, updated.shape[-1])
    total_rows = flat.shape[0]
    piece_rows = math.gcd(total_rows, 1024)
    pieces = flat.reshape(total_rows // piece_rows, piece_rows, flat.shape[1])
    pair_out = lax.map(lambda piece: transition(piece, trans_gain, w_in, w_down), pieces).reshape(
        pair.shape
    )
    return (single_out, pair_out)


MESH_ID = pl.DeviceIdType.MESH


def transposed_dot(left, right, precision=None):
    return lax.dot_general(
        left,
        right,
        (((1,), (1,)), ((), ())),
        precision=precision,
        preferred_element_type=jnp.float32,
    )


def attention_kernel(
    row_count,
    col_count,
    head_size,
    single_ref,
    embedded_ref,
    scale_ref,
    shift_ref,
    chain_ref,
    live_ref,
    pair_gain_ref,
    bias_w_ref,
    chain_bias_ref,
    gain_ref,
    left_w_ref,
    right_w_ref,
    pair_hbm,
    query_w_hbm,
    key_w_hbm,
    value_w_hbm,
    gate_w_hbm,
    out_w_hbm,
    outer_w_hbm,
    single_out_ref,
    mix_ref,
    right_ref,
    pair_ref,
    query_w_ref,
    key_w_ref,
    value_w_ref,
    gate_w_ref,
    out_w_ref,
    outer_w_ref,
    outer_wide,
    outer_flat,
    packed,
    singles,
    mods,
    biases,
    keys_values,
    gates,
    left_parts,
    right_parts,
    load_sem,
    col_send,
    col_recv,
    row_send,
    row_recv,
    right_send,
    right_recv,
):
    row_place = lax.axis_index("row")
    col_place = lax.axis_index("col")
    rows, width = single_ref.shape
    half = rows // 2
    model_width = query_w_ref.shape[1]
    factor = left_w_ref.shape[0]
    head_count = width // head_size
    all_heads = chain_bias_ref.shape[1]
    channels = pair_ref.shape[2]

    def col_peer(step):
        return {"col": lax.rem(col_place + step, col_count)}

    def row_peer(step):
        return {"row": lax.rem(row_place + step, row_count)}

    def copy(source, target, send, recv, device):
        return pltpu.make_async_remote_copy(
            src_ref=source,
            dst_ref=target,
            send_sem=send,
            recv_sem=recv,
            device_id=device,
            device_id_type=MESH_ID,
        )

    loads = [
        pltpu.make_async_copy(source, target, load_sem.at[place])
        for place, (source, target) in enumerate(
            (
                (pair_hbm, pair_ref),
                (key_w_hbm, key_w_ref),
                (value_w_hbm, value_w_ref),
                (query_w_hbm, query_w_ref),
                (gate_w_hbm, gate_w_ref),
                (out_w_hbm, out_w_ref),
                (outer_w_hbm, outer_w_ref),
            )
        )
    ]

    barrier = pltpu.get_barrier_semaphore()
    for row_step in range(row_count):
        for col_step in range(col_count):
            if row_step or col_step:
                pl.semaphore_signal(
                    barrier,
                    inc=1,
                    device_id=row_peer(row_step) | col_peer(col_step),
                    device_id_type=MESH_ID,
                )
    for each in loads:
        each.start()
    embedded = jnp.broadcast_to(embedded_ref[...], (16, embedded_ref.shape[1])).astype(jnp.bfloat16)
    mods[col_place, 0] = transposed_dot(embedded, scale_ref[...])[:8]
    mods[col_place, 1] = transposed_dot(embedded, shift_ref[...])[:8]
    singles[col_place] = single_ref[...]
    pl.semaphore_wait(barrier, row_count * col_count - 1)

    first = []
    bias_copies = []
    for step in range(1, col_count):
        peer = col_peer(step)
        first.append(
            copy(
                single_ref,
                singles.at[col_place],
                col_send.at[0, step],
                col_recv.at[0, step],
                peer,
            )
        )
        first.append(
            copy(
                mods.at[col_place],
                mods.at[col_place],
                col_send.at[1, step],
                col_recv.at[1, step],
                peer,
            )
        )
        bias_copies.append(
            copy(
                packed.at[lax.rem(col_place + step, col_count)],
                biases.at[col_place],
                col_send.at[2, step],
                col_recv.at[2, step],
                peer,
            )
        )
    for each in first:
        each.start()
    wide = row_count * rows
    spot = lax.broadcasted_iota(jnp.int32, (rows, wide), 1)
    item = lax.broadcasted_iota(jnp.int32, (rows, wide), 0)
    slot = lax.broadcasted_iota(jnp.int32, (rows, 2 * rows), 1)
    slot = jnp.where(slot >= rows, slot - rows, slot)
    entry = lax.broadcasted_iota(jnp.int32, (rows, 2 * rows), 0)

    def column(row_vector, place):
        picked = jnp.where(spot == item + place * rows, row_vector, 0.0)
        return jnp.sum(picked, axis=1, keepdims=True)

    def twice(column_vector):
        return jnp.sum(jnp.where(slot == entry, column_vector, 0.0), axis=0, keepdims=True)

    chain_all = chain_ref[...].astype(jnp.float32)
    live_all = live_ref[...].astype(jnp.float32)
    live_column = column(live_all, col_place)
    chain_query = column(chain_all, row_place)
    in_first = lax.broadcasted_iota(jnp.int32, (half, 2 * rows), 1) < rows
    chain_packed = jnp.where(in_first, chain_query[:half], chain_query[half:])
    same = chain_packed == twice(column(chain_all, col_place))
    live_term = jnp.where(twice(live_column) == 1.0, 0.0, MASKED)
    loads[0].wait()
    pair_gain = pair_gain_ref[...]
    bias_w = bias_w_ref[...]

    def score_bias(place, carry):
        tile = jnp.concatenate([pair_ref[place], pair_ref[place + half]], axis=0)
        normed = channel_norm(tile.astype(jnp.float32), pair_gain).astype(jnp.bfloat16)
        found = transposed_dot(bias_w, normed)
        for head in range(all_heads):
            packed[
                head // head_count, pl.ds((head % head_count) * half + place, 1), :
            ] = found[head : head + 1]
        return carry

    lax.fori_loop(0, half, score_bias, 0, unroll=4)
    for head in range(all_heads):
        span = pl.ds((head % head_count) * half, half)
        term = jnp.where(
            same, chain_bias_ref[0:1, head : head + 1], chain_bias_ref[1:2, head : head + 1]
        )
        packed[head // head_count, span, :] = packed[head // head_count, span, :] + term + live_term
    for each in bias_copies:
        each.start()
    biases[col_place] = packed[col_place]
    for each in first:
        each.wait()

    total = jnp.zeros((rows, 1), jnp.float32)
    squares = jnp.zeros((rows, 1), jnp.float32)
    for block in range(col_count):
        piece = singles[block].astype(jnp.float32)
        total = total + jnp.sum(piece, axis=1, keepdims=True)
        squares = squares + jnp.sum(piece * piece, axis=1, keepdims=True)
    mean = total / model_width
    inv = lax.rsqrt(squares / model_width - mean * mean + EPSILON)
    gathered = jnp.concatenate(
        [singles[block].astype(jnp.float32) for block in range(col_count)], axis=1
    )
    mod_scale = jnp.concatenate([mods[block, 0, 0:1] for block in range(col_count)], axis=1)
    mod_shift = jnp.concatenate([mods[block, 1, 0:1] for block in range(col_count)], axis=1)
    normed = (gathered - mean) * inv * (1.0 + mod_scale) + mod_shift
    normed = normed.astype(jnp.bfloat16)
    loads[1].wait()
    loads[2].wait()
    key = transposed_dot(normed, key_w_ref[...])
    value = transposed_dot(normed, value_w_ref[...])
    keys_values[row_place, 0] = key.astype(jnp.bfloat16)
    keys_values[row_place, 1] = value.astype(jnp.bfloat16)
    second = [
        copy(
            keys_values.at[row_place],
            keys_values.at[row_place],
            row_send.at[step],
            row_recv.at[step],
            row_peer(step),
        )
        for step in range(1, row_count)
    ]
    for each in second:
        each.start()
    loads[3].wait()
    loads[4].wait()
    query = transposed_dot(normed, query_w_ref[...])
    gate = transposed_dot(normed, gate_w_ref[...])
    opened = jax.nn.sigmoid(gate.astype(jnp.bfloat16).astype(jnp.float32))
    query = query.astype(jnp.bfloat16)
    lane = lax.broadcasted_iota(jnp.int32, (rows, width), 1)
    masks = [
        (lane >= head * head_size) & (lane < (head + 1) * head_size) for head in range(head_count)
    ]
    query_heads = jnp.concatenate(
        [jnp.where(mask, query, jnp.zeros_like(query)) for mask in masks], axis=0
    )
    loads[6].wait()
    outer_wide[...] = outer_w_ref[...].astype(jnp.float32)
    for place in range(factor):
        outer_flat[:, place * channels : (place + 1) * channels] = outer_wide[:, place, :].astype(
            jnp.bfloat16
        )
    for each in bias_copies:
        each.wait()
    for each in second:
        each.wait()

    def unpack(block):
        held = biases[block]
        pieces = []
        for head in range(head_count):
            part = held[head * half : (head + 1) * half]
            pieces += [part[:, :rows], part[:, rows:]]
        return jnp.concatenate(pieces, axis=0)

    scores = [
        transposed_dot(query_heads, keys_values[block, 0]) * head_size ** (-0.5) + unpack(block)
        for block in range(row_count)
    ]
    top = functools.reduce(jnp.maximum, [jnp.max(s, axis=1, keepdims=True) for s in scores])
    weights = [jnp.exp(s - top) for s in scores]
    weight_sum = sum(jnp.sum(w, axis=1, keepdims=True) for w in weights)
    summed = sum(
        jnp.dot(
            weights[block].astype(jnp.bfloat16),
            keys_values[block, 1],
            preferred_element_type=jnp.float32,
        )
        for block in range(row_count)
    )
    summed = summed / weight_sum
    attended = sum(
        jnp.where(masks[head], summed[head * rows : (head + 1) * rows], 0.0)
        for head in range(head_count)
    )
    gates[col_place] = (opened * attended).astype(jnp.bfloat16)
    third = [
        copy(
            gates.at[col_place],
            gates.at[col_place],
            col_send.at[3, step],
            col_recv.at[3, step],
            col_peer(step),
        )
        for step in range(1, col_count)
    ]
    for each in third:
        each.start()
    for each in third:
        each.wait()
    loads[5].wait()
    gated = jnp.concatenate(
        [gates[block].astype(jnp.float32) for block in range(col_count)], axis=1
    ).astype(jnp.bfloat16)
    mixed = single_ref[...].astype(jnp.float32) + transposed_dot(gated, out_w_ref[...])
    single_out = mixed.astype(jnp.bfloat16)
    single_out_ref[...] = single_out
    updated = single_out.astype(jnp.float32)
    gain = gain_ref[...]
    stacked = jnp.concatenate([updated * gain, jnp.broadcast_to(gain, (8, width))], axis=0)
    lanes = left_parts.shape[2]
    factors = jnp.concatenate(
        [
            left_w_ref[...],
            right_w_ref[...],
            jnp.zeros((lanes - 2 * factor, width), jnp.float32),
        ],
        axis=0,
    )
    products = transposed_dot(stacked, factors, lax.Precision.HIGHEST)
    place = lax.broadcasted_iota(jnp.int32, (rows, lanes), 1)
    left_parts[col_place, pl.ds(0, rows), :] = jnp.where(
        place == 2 * factor,
        jnp.sum(updated, axis=1, keepdims=True),
        jnp.where(
            place == 2 * factor + 1,
            jnp.sum(updated * updated, axis=1, keepdims=True),
            products[:rows],
        ),
    )
    left_parts[col_place, pl.ds(rows, 8), :] = products[rows:]
    fourth = [
        copy(
            left_parts.at[col_place],
            left_parts.at[col_place],
            col_send.at[4, step],
            col_recv.at[4, step],
            col_peer(step),
        )
        for step in range(1, col_count)
    ]
    right_copies = [
        copy(
            left_parts.at[col_place],
            right_parts.at[col_place],
            right_send.at[step],
            right_recv.at[col_place],
            row_peer(step) | {"col": row_place},
        )
        for step in range(row_count)
    ]
    diagonal = row_place == col_place
    for each in fourth:
        each.start()
    for step in range(1, row_count):
        right_copies[step].start()

    @pl.when(jnp.logical_not(diagonal))
    def _():
        right_copies[0].start()

    @pl.when(diagonal)
    def _():
        right_parts[col_place] = left_parts[col_place]

    for each in fourth:
        each.wait()

    def finish(parts):
        joint = parts[0]
        for block in range(1, col_count):
            joint = joint + parts[block]
        body_rows = joint[:rows]
        out_mean = body_rows[:, 2 * factor : 2 * factor + 1] / model_width
        out_square = body_rows[:, 2 * factor + 1 : 2 * factor + 2] / model_width
        out_inv = lax.rsqrt(out_square - out_mean * out_mean + EPSILON)
        return out_inv * (body_rows - out_mean * joint[rows : rows + 1])

    left = finish(left_parts)[:, :factor].astype(jnp.bfloat16)
    for which in range(factor):
        mix_ref[:, which, :] = jnp.dot(
            left,
            outer_flat[:, which * channels : (which + 1) * channels],
            preferred_element_type=jnp.float32,
        )
    for block in range(col_count):

        @pl.when(jnp.logical_not(diagonal & (col_place == block)))
        def _():
            copy(
                left_parts.at[block],
                right_parts.at[block],
                right_send.at[0],
                right_recv.at[block],
                row_peer(0),
            ).wait_recv()

    right = finish(right_parts).astype(jnp.bfloat16).astype(jnp.float32)
    right = jnp.where((place >= factor) & (place < 2 * factor), right, 0.0)
    right = jnp.where(place == 0, 1.0, right) * live_column
    right_ref[...] = (right + pltpu.roll(right, 2 * factor, 1)).astype(jnp.bfloat16)
    for step in range(1, row_count):
        right_copies[step].wait_send()

    @pl.when(jnp.logical_not(diagonal))
    def _():
        right_copies[0].wait_send()


def pair_kernel(
    live_ref,
    pair_ref,
    mix_ref,
    right_ref,
    outer_bias_ref,
    gain_ref,
    w_in_ref,
    w_down_ref,
    out_ref,
    flat_ref,
):
    block_rows, key_rows, channels = pair_ref.shape
    start = lax.axis_index("row") * key_rows + pl.program_id(0) * block_rows
    right = right_ref[...]
    factor = mix_ref.shape[1]
    top = lax.broadcasted_iota(jnp.int32, (factor, channels), 0)
    bias_rows = jnp.where(top == 0, outer_bias_ref[...], 0.0)
    for place in range(block_rows):
        terms = jnp.concatenate([bias_rows, mix_ref[place]], axis=0)
        high = terms.astype(jnp.bfloat16)
        low = (terms - high.astype(jnp.float32)).astype(jnp.bfloat16)
        outer = jnp.dot(
            right,
            jnp.concatenate([high, low], axis=0),
            preferred_element_type=jnp.float32,
        )
        outer = outer * live_ref[start + place].astype(jnp.float32)
        flat_ref[pl.ds(place * key_rows, key_rows), :] = pair_ref[place].astype(jnp.float32) + outer
    flat = flat_ref[...]
    normed = channel_norm(flat, gain_ref[...]).astype(jnp.bfloat16)
    hidden_width = w_down_ref.shape[0]
    chunk = math.gcd(hidden_width, 256)
    result = flat
    for first in range(0, hidden_width, chunk):
        gate = jnp.dot(normed, w_in_ref[:, first : first + chunk], preferred_element_type=jnp.float32)
        up = jnp.dot(
            normed,
            w_in_ref[:, hidden_width + first : hidden_width + first + chunk],
            preferred_element_type=jnp.float32,
        )
        half = gate * 0.5
        hidden = ((half + half * jnp.tanh(half)) * up).astype(jnp.bfloat16)
        result = result + jnp.dot(
            hidden, w_down_ref[first : first + chunk, :], preferred_element_type=jnp.float32
        )
    out_ref[...] = result.astype(jnp.bfloat16).reshape(out_ref.shape)


def fast_body(
    row_count,
    col_count,
    single,
    pair,
    chain,
    live,
    step_index,
    time_scale,
    time_shift,
    w_query,
    w_key,
    w_value,
    w_gate,
    w_out,
    pair_gain,
    bias_weight,
    chain_bias,
    outer_gain,
    w_left,
    w_right,
    w_outer,
    outer_bias,
    trans_gain,
    w_in,
    w_down,
):
    rows, width = single.shape
    model_width = w_query.shape[0]
    head_count = chain_bias.shape[1]
    head_size = model_width // head_count
    local_heads = head_count // col_count
    factor = w_left.shape[1]
    channels = pair.shape[2]
    embedded = time_embed(step_index, time_scale.shape[0]).astype(jnp.bfloat16)
    lanes = 4 * factor
    tile_heads = 16 * pl.cdiv(head_count, 16)
    bias_w = jnp.pad(bias_weight.T, ((0, tile_heads - head_count), (0, 0)))
    vmem = pl.BlockSpec(memory_space=pltpu.VMEM)
    bf16, f32 = jnp.bfloat16, jnp.float32
    hbm = pl.BlockSpec(memory_space=pl.ANY)
    weight = pltpu.VMEM((width, model_width), bf16)
    single_out, mix, right = pl.pallas_call(
        functools.partial(attention_kernel, row_count, col_count, head_size),
        out_shape=(
            jax.ShapeDtypeStruct((rows, width), bf16),
            jax.ShapeDtypeStruct((rows, factor, channels), f32),
            jax.ShapeDtypeStruct((rows, lanes), bf16),
        ),
        in_specs=[vmem] * 12 + [hbm] * 7,
        out_specs=(vmem, vmem, vmem),
        scratch_shapes=[
            pltpu.VMEM(pair.shape, bf16),
            weight,
            weight,
            weight,
            weight,
            weight,
            pltpu.VMEM(w_outer.shape, bf16),
            pltpu.VMEM(w_outer.shape, f32),
            pltpu.VMEM((factor, factor * channels), bf16),
            pltpu.VMEM((col_count, local_heads * rows // 2, 2 * rows), f32),
            pltpu.VMEM((col_count, rows, width), bf16),
            pltpu.VMEM((col_count, 2, 8, width), f32),
            pltpu.VMEM((col_count, local_heads * rows // 2, 2 * rows), f32),
            pltpu.VMEM((row_count, 2, rows, width), bf16),
            pltpu.VMEM((col_count, rows, width), bf16),
            pltpu.VMEM((col_count, rows + 8, lanes), f32),
            pltpu.VMEM((col_count, rows + 8, lanes), f32),
            pltpu.SemaphoreType.DMA((7,)),
            pltpu.SemaphoreType.DMA((5, col_count)),
            pltpu.SemaphoreType.DMA((5, col_count)),
            pltpu.SemaphoreType.DMA((row_count,)),
            pltpu.SemaphoreType.DMA((row_count,)),
            pltpu.SemaphoreType.DMA((row_count,)),
            pltpu.SemaphoreType.DMA((col_count,)),
        ],
        compiler_params=pltpu.CompilerParams(collective_id=0, has_side_effects=True),
        name="attention",
    )(
        single,
        embedded[None].astype(f32),
        time_scale.T,
        time_shift.T,
        chain[None],
        live[None],
        pair_gain[None],
        bias_w,
        chain_bias,
        outer_gain[None],
        w_left.T,
        w_right.T,
        pair,
        w_query.T,
        w_key.T,
        w_value.T,
        w_gate.T,
        w_out.T,
        w_outer,
    )
    block = math.gcd(rows, 8)
    hidden = w_down.shape[0]
    pair_out = pl.pallas_call(
        pair_kernel,
        grid=(rows // block,),
        out_shape=jax.ShapeDtypeStruct(pair.shape, bf16),
        in_specs=[
            pl.BlockSpec(memory_space=pltpu.SMEM),
            pl.BlockSpec((block, rows, channels), lambda i: (i, 0, 0)),
            pl.BlockSpec((block, factor, channels), lambda i: (i, 0, 0)),
            pl.BlockSpec((rows, lanes), lambda i: (0, 0)),
            pl.BlockSpec((1, channels), lambda i: (0, 0)),
            pl.BlockSpec((1, channels), lambda i: (0, 0)),
            pl.BlockSpec((channels, 2 * hidden), lambda i: (0, 0)),
            pl.BlockSpec((hidden, channels), lambda i: (0, 0)),
        ],
        out_specs=pl.BlockSpec((block, rows, channels), lambda i: (i, 0, 0)),
        scratch_shapes=[pltpu.VMEM((block * rows, channels), f32)],
        name="transition",
    )(
        live,
        pair,
        mix,
        right,
        outer_bias[None],
        trans_gain[None],
        w_in,
        w_down,
    )
    return (single_out, pair_out)


def solution(mesh):
    in_specs = (
        P(("groups", "row"), "col"),
        P(("groups", "row"), "col", None),
        P("groups"),
        P("groups"),
        P("groups"),
        P(None, "col"),
        P(None, "col"),
        P(None, "col"),
        P(None, "col"),
        P(None, "col"),
        P(None, "col"),
        P(None, "col"),
        P(),
        P(),
        P(),
        P("col"),
        P("col", None),
        P("col", None),
        P(),
        P(),
        P(),
        P(),
        P(),
    )
    out_specs = (P(("groups", "row"), "col"), P(("groups", "row"), "col", None))
    row_count, col_count = mesh.shape["row"], mesh.shape["col"]

    def chosen(*args):
        head_count = args[14].shape[1]
        if row_count == col_count and head_count % col_count == 0:
            return fast_body(row_count, col_count, *args)
        return body(*args)

    return jax.shard_map(chosen, mesh=mesh, in_specs=in_specs, out_specs=out_specs, check_vma=False)
```

```python
import functools
import math

import jax
import jax.numpy as jnp
from jax import lax
from jax.experimental import pallas as pl
from jax.experimental.pallas import tpu as pltpu
from jax.sharding import PartitionSpec as P

EPSILON = 1e-05
MASKED = -1000000000.0


def broadcast(array, axis, root):
    mine = lax.axis_index(axis) == root
    return lax.psum(jnp.where(mine, array, jnp.zeros_like(array)), axis)


def channel_norm(values, gain):
    row_mean = jnp.mean(values, axis=-1, keepdims=True)
    spread = jnp.mean(values * values, axis=-1, keepdims=True) - row_mean * row_mean
    return (values - row_mean) * lax.rsqrt(spread + EPSILON) * gain


def time_embed(step_index, count):
    halfway = count // 2
    ladder = jnp.arange(halfway).astype(jnp.float32)
    freqs = jnp.exp(-math.log(10000.0) * ladder / halfway)
    angles = step_index[0].astype(jnp.float32) * freqs
    return jnp.concatenate([jnp.sin(angles), jnp.cos(angles)])


def head_scores(query_rows, key_rows, bias_terms, head_count):
    query_heads = query_rows.reshape(query_rows.shape[0], head_count, -1)
    key_heads = key_rows.reshape(key_rows.shape[0], head_count, -1)
    raw = jnp.einsum("qhd,khd->hqk", query_heads, key_heads, preferred_element_type=jnp.float32)
    return raw * query_heads.shape[2] ** (-0.5) + bias_terms


def weighted_values(weights_exp, value_rows, head_count):
    value_heads = value_rows.reshape(value_rows.shape[0], head_count, -1).astype(jnp.float32)
    summed = jnp.einsum("hqk,khd->qhd", weights_exp, value_heads, precision=lax.Precision.HIGHEST)
    return summed.reshape(summed.shape[0], -1)


def divide_heads(summed, totals):
    row_count = summed.shape[0]
    head_count = totals.shape[0]
    return (summed.reshape(row_count, head_count, -1) / totals.T[:, :, None]).reshape(row_count, -1)


def transition(flat, gain, w_in, w_down):
    normed = channel_norm(flat, gain).astype(jnp.bfloat16)
    mixed = jnp.dot(normed, w_in, preferred_element_type=jnp.float32)
    halfway = w_down.shape[0]
    hidden = (jax.nn.silu(mixed[:, :halfway]) * mixed[:, halfway:]).astype(jnp.bfloat16)
    return (flat + jnp.dot(hidden, w_down, preferred_element_type=jnp.float32)).astype(jnp.bfloat16)


def body(
    single,
    pair,
    chain,
    live,
    step_index,
    time_scale,
    time_shift,
    w_query,
    w_key,
    w_value,
    w_gate,
    w_out,
    pair_gain,
    bias_weight,
    chain_bias,
    outer_gain,
    w_left,
    w_right,
    w_outer,
    outer_bias,
    trans_gain,
    w_in,
    w_down,
):
    block_rows = single.shape[0]
    model_width = w_query.shape[0]
    head_count = chain_bias.shape[1]
    row_place = lax.axis_index("row")
    col_place = lax.axis_index("col")
    query_start = row_place * block_rows
    key_start = col_place * block_rows
    chain_query = lax.dynamic_slice_in_dim(chain, query_start, block_rows, 0)
    chain_key = lax.dynamic_slice_in_dim(chain, key_start, block_rows, 0)
    live_query = lax.dynamic_slice_in_dim(live, query_start, block_rows, 0).astype(jnp.float32)
    live_keys = lax.dynamic_slice_in_dim(live, key_start, block_rows, 0)
    single_f = single.astype(jnp.float32)
    totals = lax.psum((jnp.sum(single_f, axis=1), jnp.sum(single_f * single_f, axis=1)), "col")
    row_mean = totals[0] / model_width
    inv_std = lax.rsqrt(totals[1] / model_width - row_mean * row_mean + EPSILON)
    embedded = time_embed(step_index, time_scale.shape[0]).astype(jnp.bfloat16)
    mod_scale = jnp.dot(embedded[None], time_scale, preferred_element_type=jnp.float32)[0]
    mod_shift = jnp.dot(embedded[None], time_shift, preferred_element_type=jnp.float32)[0]
    normed = (
        (single_f - row_mean[:, None]) * inv_std[:, None] * (1.0 + mod_scale) + mod_shift
    ).astype(jnp.bfloat16)
    normed_full = lax.all_gather(normed, "col", axis=1, tiled=True)
    query_part = jnp.dot(normed_full, w_query, preferred_element_type=jnp.float32).astype(
        jnp.bfloat16
    )
    key_part = jnp.dot(normed_full, w_key, preferred_element_type=jnp.float32).astype(jnp.bfloat16)
    value_part = jnp.dot(normed_full, w_value, preferred_element_type=jnp.float32).astype(
        jnp.bfloat16
    )
    gate_part = jnp.dot(normed_full, w_gate, preferred_element_type=jnp.float32).astype(
        jnp.bfloat16
    )
    query_full, key_full, value_full, gate_full = (
        lax.all_gather(query_part, "col", axis=1, tiled=True),
        lax.all_gather(key_part, "col", axis=1, tiled=True),
        lax.all_gather(value_part, "col", axis=1, tiled=True),
        lax.all_gather(gate_part, "col", axis=1, tiled=True),
    )
    key_cols, value_cols = (
        broadcast(key_full, "row", col_place),
        broadcast(value_full, "row", col_place),
    )
    pair_normed = channel_norm(pair.astype(jnp.float32), pair_gain).astype(jnp.bfloat16)
    bias_terms = jnp.einsum(
        "qkc,ch->hqk", pair_normed, bias_weight, preferred_element_type=jnp.float32
    )
    same_chain = chain_query[:, None] == chain_key[None, :]
    chain_terms = jnp.where(
        same_chain[None], chain_bias[0][:, None, None], chain_bias[1][:, None, None]
    )
    live_terms = jnp.where(live_keys == 1, 0.0, MASKED).astype(jnp.float32)
    bias_terms = bias_terms + chain_terms + live_terms[None, None, :]
    scores = head_scores(query_full, key_cols, bias_terms, head_count)
    row_top = lax.pmax(jnp.max(scores, axis=2), "col")
    weights_exp = jnp.exp(scores - row_top[:, :, None])
    row_sum, summed = lax.psum(
        (jnp.sum(weights_exp, axis=2), weighted_values(weights_exp, value_cols, head_count)), "col"
    )
    attended = divide_heads(summed, row_sum)
    gated = (jax.nn.sigmoid(gate_full.astype(jnp.float32)) * attended).astype(jnp.bfloat16)
    single_out = (single_f + jnp.dot(gated, w_out, preferred_element_type=jnp.float32)).astype(
        jnp.bfloat16
    )
    updated_single = single_out.astype(jnp.float32)
    gained = updated_single * outer_gain
    joint = lax.psum(
        (
            jnp.sum(updated_single, axis=1),
            jnp.sum(updated_single * updated_single, axis=1),
            jnp.dot(gained, w_left, precision=lax.Precision.HIGHEST),
            jnp.dot(gained, w_right, precision=lax.Precision.HIGHEST),
            jnp.dot(outer_gain[None], w_left, precision=lax.Precision.HIGHEST)[0],
            jnp.dot(outer_gain[None], w_right, precision=lax.Precision.HIGHEST)[0],
        ),
        "col",
    )
    out_mean = joint[0] / model_width
    out_inv = lax.rsqrt(joint[1] / model_width - out_mean * out_mean + EPSILON)
    left_full = out_inv[:, None] * (joint[2] - out_mean[:, None] * joint[4][None, :])
    right_full = out_inv[:, None] * (joint[3] - out_mean[:, None] * joint[5][None, :])
    left_rows = left_full.astype(jnp.bfloat16)
    right_rows = right_full.astype(jnp.bfloat16)
    right_cols = broadcast(right_rows, "row", col_place)
    left_mix = jnp.einsum("ip,pqc->iqc", left_rows, w_outer, preferred_element_type=jnp.float32)
    outer = (
        jnp.einsum(
            "iqc,jq->ijc", left_mix, right_cols.astype(jnp.float32), precision=lax.Precision.HIGHEST
        )
        + outer_bias
    )
    outer = outer * (live_query[:, None] * live_keys.astype(jnp.float32)[None, :])[:, :, None]
    updated = pair.astype(jnp.float32) + outer
    flat = updated.reshape(-1, updated.shape[-1])
    total_rows = flat.shape[0]
    piece_rows = math.gcd(total_rows, 1024)
    pieces = flat.reshape(total_rows // piece_rows, piece_rows, flat.shape[1])
    pair_out = lax.map(lambda piece: transition(piece, trans_gain, w_in, w_down), pieces).reshape(
        pair.shape
    )
    return (single_out, pair_out)


MESH_ID = pl.DeviceIdType.MESH


def transposed_dot(left, right, precision=None):
    return lax.dot_general(
        left,
        right,
        (((1,), (1,)), ((), ())),
        precision=precision,
        preferred_element_type=jnp.float32,
    )


def pack(values):
    rows, width = values.shape
    whole = width - width % 128
    if rows % 32 or 2 * (width - whole) != 128:
        return values
    half = rows // 2
    rest = jnp.concatenate([values[:half, whole:], values[half:, whole:]], axis=1)
    columns = [values[:, place : place + 128] for place in range(0, whole, 128)]
    return jnp.concatenate(columns + [rest], axis=0)


def unpack(held, rows, width):
    whole = width - width % 128
    if held.shape == (rows, width):
        return held
    rest = held[(whole // 128) * rows :]
    rest = jnp.concatenate([rest[:, :64], rest[:, 64:]], axis=0)
    columns = [held[place * rows : (place + 1) * rows] for place in range(whole // 128)]
    return jnp.concatenate(columns + [rest], axis=1)


def attention_kernel(
    row_count,
    col_count,
    head_size,
    single_ref,
    embedded_ref,
    scale_ref,
    shift_ref,
    chain_ref,
    live_ref,
    pair_gain_ref,
    bias_w_ref,
    chain_bias_ref,
    gain_ref,
    left_w_ref,
    right_w_ref,
    pair_hbm,
    query_w_hbm,
    key_w_hbm,
    value_w_hbm,
    gate_w_hbm,
    out_w_hbm,
    outer_w_hbm,
    single_out_ref,
    mix_ref,
    right_ref,
    pair_ref,
    query_w_ref,
    key_w_ref,
    value_w_ref,
    gate_w_ref,
    out_w_ref,
    outer_w_ref,
    outer_wide,
    outer_flat,
    packed,
    singles,
    mods,
    biases,
    keys_values,
    gates,
    left_parts,
    right_parts,
    own_right,
    load_sem,
    col_send,
    col_recv,
    row_send,
    row_recv,
    right_send,
    right_recv,
):
    row_place = lax.axis_index("row")
    col_place = lax.axis_index("col")
    rows, width = single_ref.shape
    half = rows // 2
    model_width = query_w_ref.shape[1]
    factor = left_w_ref.shape[0]
    head_count = width // head_size
    all_heads = chain_bias_ref.shape[1]
    channels = pair_ref.shape[2]

    def col_peer(step):
        return {"col": lax.rem(col_place + step, col_count)}

    def row_peer(step):
        return {"row": lax.rem(row_place + step, row_count)}

    def copy(source, target, send, recv, device):
        return pltpu.make_async_remote_copy(
            src_ref=source,
            dst_ref=target,
            send_sem=send,
            recv_sem=recv,
            device_id=device,
            device_id_type=MESH_ID,
        )

    loads = [
        pltpu.make_async_copy(source, target, load_sem.at[place])
        for place, (source, target) in enumerate(
            (
                (pair_hbm, pair_ref),
                (key_w_hbm, key_w_ref),
                (value_w_hbm, value_w_ref),
                (query_w_hbm, query_w_ref),
                (gate_w_hbm, gate_w_ref),
                (out_w_hbm, out_w_ref),
                (outer_w_hbm, outer_w_ref),
            )
        )
    ]

    barrier = pltpu.get_barrier_semaphore()
    for row_step in range(row_count):
        for col_step in range(col_count):
            if row_step or col_step:
                pl.semaphore_signal(
                    barrier,
                    inc=1,
                    device_id=row_peer(row_step) | col_peer(col_step),
                    device_id_type=MESH_ID,
                )
    for each in loads:
        each.start()
    embedded = jnp.broadcast_to(embedded_ref[...], (16, embedded_ref.shape[1])).astype(jnp.bfloat16)
    mod_scale = transposed_dot(embedded, scale_ref[...])[:8]
    mod_shift = transposed_dot(embedded, shift_ref[...])[:8]
    mod_row = lax.broadcasted_iota(jnp.int32, mod_scale.shape, 0)
    mods[col_place] = jnp.where(mod_row == 0, mod_scale, mod_shift)
    singles[col_place] = pack(single_ref[...].astype(jnp.float32)).astype(jnp.bfloat16)
    pl.semaphore_wait(barrier, row_count * col_count - 1)

    first = []
    bias_copies = []
    for step in range(1, col_count):
        peer = col_peer(step)
        first.append(
            copy(
                singles.at[col_place],
                singles.at[col_place],
                col_send.at[0, step],
                col_recv.at[0, step],
                peer,
            )
        )
        first.append(
            copy(
                mods.at[col_place],
                mods.at[col_place],
                col_send.at[1, step],
                col_recv.at[1, step],
                peer,
            )
        )
        bias_copies.append(
            copy(
                packed.at[lax.rem(col_place + step, col_count)],
                biases.at[col_place],
                col_send.at[2, step],
                col_recv.at[2, step],
                peer,
            )
        )
    for each in first:
        each.start()
    wide = row_count * rows
    spot = lax.broadcasted_iota(jnp.int32, (rows, wide), 1)
    item = lax.broadcasted_iota(jnp.int32, (rows, wide), 0)
    slot = lax.broadcasted_iota(jnp.int32, (rows, 2 * rows), 1)
    slot = jnp.where(slot >= rows, slot - rows, slot)
    entry = lax.broadcasted_iota(jnp.int32, (rows, 2 * rows), 0)

    def column(row_vector, place):
        picked = jnp.where(spot == item + place * rows, row_vector, 0.0)
        return jnp.sum(picked, axis=1, keepdims=True)

    def twice(column_vector):
        return jnp.sum(jnp.where(slot == entry, column_vector, 0.0), axis=0, keepdims=True)

    chain_all = chain_ref[...].astype(jnp.float32)
    live_all = live_ref[...].astype(jnp.float32)
    live_column = column(live_all, col_place)
    chain_query = column(chain_all, row_place)
    in_first = lax.broadcasted_iota(jnp.int32, (half, 2 * rows), 1) < rows
    chain_packed = jnp.where(in_first, chain_query[:half], chain_query[half:])
    same = chain_packed == twice(column(chain_all, col_place))
    live_term = jnp.where(twice(live_column) == 1.0, 0.0, MASKED)
    loads[0].wait()
    pair_gain = pair_gain_ref[...]
    bias_w = bias_w_ref[...]

    def score_bias(place, carry):
        tile = jnp.concatenate([pair_ref[place], pair_ref[place + half]], axis=0)
        normed = channel_norm(tile.astype(jnp.float32), pair_gain).astype(jnp.bfloat16)
        found = transposed_dot(bias_w, normed)
        for head in range(all_heads):
            packed[
                head // head_count, pl.ds((head % head_count) * half + place, 1), :
            ] = found[head : head + 1]
        return carry

    lax.fori_loop(0, half, score_bias, 0, unroll=4)
    for head in range(all_heads):
        span = pl.ds((head % head_count) * half, half)
        term = jnp.where(
            same, chain_bias_ref[0:1, head : head + 1], chain_bias_ref[1:2, head : head + 1]
        )
        packed[head // head_count, span, :] = packed[head // head_count, span, :] + term + live_term
    for each in bias_copies:
        each.start()
    biases[col_place] = packed[col_place]
    for each in first:
        each.wait()

    gathered = jnp.concatenate(
        [unpack(singles[block].astype(jnp.float32), rows, width) for block in range(col_count)],
        axis=1,
    )
    mod_scale = jnp.concatenate([mods[block, 0:1] for block in range(col_count)], axis=1)
    mod_shift = jnp.concatenate([mods[block, 1:2] for block in range(col_count)], axis=1)
    total = jnp.sum(gathered, axis=1, keepdims=True)
    squares = jnp.sum(gathered * gathered, axis=1, keepdims=True)
    mean = total / model_width
    inv = lax.rsqrt(squares / model_width - mean * mean + EPSILON)
    normed = (gathered - mean) * inv * (1.0 + mod_scale) + mod_shift
    normed = normed.astype(jnp.bfloat16)
    loads[1].wait()
    loads[2].wait()
    key = transposed_dot(normed, key_w_ref[...])
    value = transposed_dot(normed, value_w_ref[...])
    keys_values[row_place, 0] = key.astype(jnp.bfloat16)
    keys_values[row_place, 1] = value.astype(jnp.bfloat16)
    second = [
        copy(
            keys_values.at[row_place],
            keys_values.at[row_place],
            row_send.at[step],
            row_recv.at[step],
            row_peer(step),
        )
        for step in range(1, row_count)
    ]
    for each in second:
        each.start()
    loads[3].wait()
    loads[4].wait()
    query = transposed_dot(normed, query_w_ref[...])
    gate = transposed_dot(normed, gate_w_ref[...])
    opened = jax.nn.sigmoid(gate.astype(jnp.bfloat16).astype(jnp.float32))
    query = query.astype(jnp.bfloat16)
    lane = lax.broadcasted_iota(jnp.int32, (rows, width), 1)
    masks = [
        (lane >= head * head_size) & (lane < (head + 1) * head_size) for head in range(head_count)
    ]
    query_heads = jnp.concatenate(
        [jnp.where(mask, query, jnp.zeros_like(query)) for mask in masks], axis=0
    )
    loads[6].wait()
    outer_wide[...] = outer_w_ref[...].astype(jnp.float32)
    for place in range(factor):
        outer_flat[:, place * channels : (place + 1) * channels] = outer_wide[:, place, :].astype(
            jnp.bfloat16
        )
    for each in bias_copies:
        each.wait()
    for each in second:
        each.wait()

    def unpack_bias(block):
        held = biases[block]
        pieces = []
        for head in range(head_count):
            part = held[head * half : (head + 1) * half]
            pieces += [part[:, :rows], part[:, rows:]]
        return jnp.concatenate(pieces, axis=0)

    scores = [
        transposed_dot(query_heads, keys_values[block, 0]) * head_size ** (-0.5) + unpack_bias(block)
        for block in range(row_count)
    ]
    top = functools.reduce(jnp.maximum, [jnp.max(s, axis=1, keepdims=True) for s in scores])
    weights = [jnp.exp(s - top) for s in scores]
    weight_sum = sum(jnp.sum(w, axis=1, keepdims=True) for w in weights)
    summed = sum(
        jnp.dot(
            weights[block].astype(jnp.bfloat16),
            keys_values[block, 1],
            preferred_element_type=jnp.float32,
        )
        for block in range(row_count)
    )
    summed = summed / weight_sum
    attended = sum(
        jnp.where(masks[head], summed[head * rows : (head + 1) * rows], 0.0)
        for head in range(head_count)
    )
    gates[col_place] = pack(opened * attended).astype(jnp.bfloat16)
    third = [
        copy(
            gates.at[col_place],
            gates.at[col_place],
            col_send.at[3, step],
            col_recv.at[3, step],
            col_peer(step),
        )
        for step in range(1, col_count)
    ]
    for each in third:
        each.start()
    for each in third:
        each.wait()
    loads[5].wait()
    gated = jnp.concatenate(
        [unpack(gates[block].astype(jnp.float32), rows, width) for block in range(col_count)],
        axis=1,
    ).astype(jnp.bfloat16)
    mixed = single_ref[...].astype(jnp.float32) + transposed_dot(gated, out_w_ref[...])
    single_out = mixed.astype(jnp.bfloat16)
    single_out_ref[...] = single_out
    updated = single_out.astype(jnp.float32)
    gain = gain_ref[...]
    precise = lax.Precision.HIGHEST
    factors = jnp.concatenate([left_w_ref[...], right_w_ref[...]], axis=0)
    products = transposed_dot(factors, updated * gain, precise)
    ones = jnp.ones((8, width), jnp.float32)
    totals = jnp.concatenate(
        [
            transposed_dot(ones, updated, precise),
            transposed_dot(ones, updated * updated, precise),
        ],
        axis=1,
    )
    weight_sums = transposed_dot(jnp.broadcast_to(gain, (8, width)), factors, precise)
    weight_sums = jnp.concatenate([weight_sums, jnp.zeros_like(totals[:, 2 * factor :])], axis=1)
    stat_row = lax.broadcasted_iota(jnp.int32, totals.shape, 0)
    statistics = jnp.where(stat_row == 0, totals, weight_sums)
    part = factor // 2
    for parts, start in ((left_parts, 0), (own_right, factor)):
        sides = [products[start : start + part], products[start + part : start + factor]]
        joined = jnp.concatenate([jnp.concatenate(sides, axis=1), statistics], axis=0)
        if parts is left_parts:
            parts[col_place] = joined
        else:
            parts[...] = joined
    fourth = [
        copy(
            left_parts.at[col_place],
            left_parts.at[col_place],
            col_send.at[4, step],
            col_recv.at[4, step],
            col_peer(step),
        )
        for step in range(1, col_count)
    ]
    right_copies = [
        copy(
            own_right,
            right_parts.at[col_place],
            right_send.at[step],
            right_recv.at[col_place],
            row_peer(step) | {"col": row_place},
        )
        for step in range(row_count)
    ]
    diagonal = row_place == col_place
    for each in fourth:
        each.start()
    for step in range(1, row_count):
        right_copies[step].start()

    @pl.when(jnp.logical_not(diagonal))
    def _():
        right_copies[0].start()

    @pl.when(diagonal)
    def _():
        right_parts[col_place] = own_right[...]

    for each in fourth:
        each.wait()

    which_factor = lax.broadcasted_iota(jnp.int32, (factor, 2 * rows), 0)
    which_lane = lax.broadcasted_iota(jnp.int32, (factor, 2 * rows), 1)

    def finish(parts, start):
        joint = parts[0]
        for block in range(1, col_count):
            joint = joint + parts[block]
        out_mean = joint[part : part + 1, :rows] / model_width
        out_square = joint[part : part + 1, rows:] / model_width
        out_inv = lax.rsqrt(out_square - out_mean * out_mean + EPSILON)
        picked = jnp.where(which_lane == which_factor + start, joint[part + 1 : part + 2], 0.0)
        sums = jnp.sum(picked, axis=1, keepdims=True)
        body_rows = jnp.concatenate([joint[:part, :rows], joint[:part, rows:]], axis=0)
        return out_inv * (body_rows - out_mean * sums)

    left = finish(left_parts, 0).T.astype(jnp.bfloat16)
    for which in range(factor):
        mix_ref[:, which, :] = jnp.dot(
            left,
            outer_flat[:, which * channels : (which + 1) * channels],
            preferred_element_type=jnp.float32,
        )
    for block in range(col_count):

        @pl.when(jnp.logical_not(diagonal & (col_place == block)))
        def _():
            copy(
                own_right,
                right_parts.at[block],
                right_send.at[0],
                right_recv.at[block],
                row_peer(0),
            ).wait_recv()

    right = finish(right_parts, factor).astype(jnp.bfloat16).astype(jnp.float32)
    top = jnp.where(lax.broadcasted_iota(jnp.int32, right.shape, 0) == 0, 1.0, 0.0)
    right = jnp.concatenate([top, right, top, right], axis=0).T * live_column
    right_ref[...] = right.astype(jnp.bfloat16)
    for step in range(1, row_count):
        right_copies[step].wait_send()

    @pl.when(jnp.logical_not(diagonal))
    def _():
        right_copies[0].wait_send()


def pair_kernel(
    live_ref,
    pair_ref,
    mix_ref,
    right_ref,
    outer_bias_ref,
    gain_ref,
    w_in_ref,
    w_down_ref,
    out_ref,
    flat_ref,
):
    block_rows, key_rows, channels = pair_ref.shape
    start = lax.axis_index("row") * key_rows + pl.program_id(0) * block_rows
    right = right_ref[...]
    factor = mix_ref.shape[1]
    top = lax.broadcasted_iota(jnp.int32, (factor, channels), 0)
    bias_rows = jnp.where(top == 0, outer_bias_ref[...], 0.0)
    for place in range(block_rows):
        terms = jnp.concatenate([bias_rows, mix_ref[place]], axis=0)
        high = terms.astype(jnp.bfloat16)
        low = (terms - high.astype(jnp.float32)).astype(jnp.bfloat16)
        outer = jnp.dot(
            right,
            jnp.concatenate([high, low], axis=0),
            preferred_element_type=jnp.float32,
        )
        outer = outer * live_ref[start + place].astype(jnp.float32)
        flat_ref[pl.ds(place * key_rows, key_rows), :] = pair_ref[place].astype(jnp.float32) + outer
    flat = flat_ref[...]
    normed = channel_norm(flat, gain_ref[...]).astype(jnp.bfloat16)
    hidden_width = w_down_ref.shape[0]
    chunk = math.gcd(hidden_width, 256)
    result = flat
    for first in range(0, hidden_width, chunk):
        gate = jnp.dot(normed, w_in_ref[:, first : first + chunk], preferred_element_type=jnp.float32)
        up = jnp.dot(
            normed,
            w_in_ref[:, hidden_width + first : hidden_width + first + chunk],
            preferred_element_type=jnp.float32,
        )
        half = gate * 0.5
        hidden = ((half + half * jnp.tanh(half)) * up).astype(jnp.bfloat16)
        result = result + jnp.dot(
            hidden, w_down_ref[first : first + chunk, :], preferred_element_type=jnp.float32
        )
    out_ref[...] = result.astype(jnp.bfloat16).reshape(out_ref.shape)


def fast_body(
    row_count,
    col_count,
    single,
    pair,
    chain,
    live,
    step_index,
    time_scale,
    time_shift,
    w_query,
    w_key,
    w_value,
    w_gate,
    w_out,
    pair_gain,
    bias_weight,
    chain_bias,
    outer_gain,
    w_left,
    w_right,
    w_outer,
    outer_bias,
    trans_gain,
    w_in,
    w_down,
):
    rows, width = single.shape
    model_width = w_query.shape[0]
    head_count = chain_bias.shape[1]
    head_size = model_width // head_count
    local_heads = head_count // col_count
    factor = w_left.shape[1]
    channels = pair.shape[2]
    embedded = time_embed(step_index, time_scale.shape[0]).astype(jnp.bfloat16)
    lanes = 4 * factor
    tile_heads = 16 * pl.cdiv(head_count, 16)
    bias_w = jnp.pad(bias_weight.T, ((0, tile_heads - head_count), (0, 0)))
    vmem = pl.BlockSpec(memory_space=pltpu.VMEM)
    bf16, f32 = jnp.bfloat16, jnp.float32
    packed_shape = jax.eval_shape(pack, jax.ShapeDtypeStruct((rows, width), f32)).shape
    hbm = pl.BlockSpec(memory_space=pl.ANY)
    weight = pltpu.VMEM((width, model_width), bf16)
    single_out, mix, right = pl.pallas_call(
        functools.partial(attention_kernel, row_count, col_count, head_size),
        out_shape=(
            jax.ShapeDtypeStruct((rows, width), bf16),
            jax.ShapeDtypeStruct((rows, factor, channels), f32),
            jax.ShapeDtypeStruct((rows, lanes), bf16),
        ),
        in_specs=[vmem] * 12 + [hbm] * 7,
        out_specs=(vmem, vmem, vmem),
        scratch_shapes=[
            pltpu.VMEM(pair.shape, bf16),
            weight,
            weight,
            weight,
            weight,
            weight,
            pltpu.VMEM(w_outer.shape, bf16),
            pltpu.VMEM(w_outer.shape, f32),
            pltpu.VMEM((factor, factor * channels), bf16),
            pltpu.VMEM((col_count, local_heads * rows // 2, 2 * rows), f32),
            pltpu.VMEM((col_count,) + packed_shape, bf16),
            pltpu.VMEM((col_count, 8, width), f32),
            pltpu.VMEM((col_count, local_heads * rows // 2, 2 * rows), f32),
            pltpu.VMEM((row_count, 2, rows, width), bf16),
            pltpu.VMEM((col_count,) + packed_shape, bf16),
            pltpu.VMEM((col_count, factor // 2 + 8, 2 * rows), f32),
            pltpu.VMEM((col_count, factor // 2 + 8, 2 * rows), f32),
            pltpu.VMEM((factor // 2 + 8, 2 * rows), f32),
            pltpu.SemaphoreType.DMA((7,)),
            pltpu.SemaphoreType.DMA((5, col_count)),
            pltpu.SemaphoreType.DMA((5, col_count)),
            pltpu.SemaphoreType.DMA((row_count,)),
            pltpu.SemaphoreType.DMA((row_count,)),
            pltpu.SemaphoreType.DMA((row_count,)),
            pltpu.SemaphoreType.DMA((col_count,)),
        ],
        compiler_params=pltpu.CompilerParams(collective_id=0, has_side_effects=True),
        name="attention",
    )(
        single,
        embedded[None].astype(f32),
        time_scale.T,
        time_shift.T,
        chain[None],
        live[None],
        pair_gain[None],
        bias_w,
        chain_bias,
        outer_gain[None],
        w_left.T,
        w_right.T,
        pair,
        w_query.T,
        w_key.T,
        w_value.T,
        w_gate.T,
        w_out.T,
        w_outer,
    )
    block = math.gcd(rows, 32)
    hidden = w_down.shape[0]
    pair_out = pl.pallas_call(
        pair_kernel,
        grid=(rows // block,),
        out_shape=jax.ShapeDtypeStruct(pair.shape, bf16),
        in_specs=[
            pl.BlockSpec(memory_space=pltpu.SMEM),
            pl.BlockSpec((block, rows, channels), lambda i: (i, 0, 0)),
            pl.BlockSpec((block, factor, channels), lambda i: (i, 0, 0)),
            pl.BlockSpec((rows, lanes), lambda i: (0, 0)),
            pl.BlockSpec((1, channels), lambda i: (0, 0)),
            pl.BlockSpec((1, channels), lambda i: (0, 0)),
            pl.BlockSpec((channels, 2 * hidden), lambda i: (0, 0)),
            pl.BlockSpec((hidden, channels), lambda i: (0, 0)),
        ],
        out_specs=pl.BlockSpec((block, rows, channels), lambda i: (i, 0, 0)),
        scratch_shapes=[pltpu.VMEM((block * rows, channels), f32)],
        name="transition",
    )(
        live,
        pair,
        mix,
        right,
        outer_bias[None],
        trans_gain[None],
        w_in,
        w_down,
    )
    return (single_out, pair_out)


def solution(mesh):
    in_specs = (
        P(("groups", "row"), "col"),
        P(("groups", "row"), "col", None),
        P("groups"),
        P("groups"),
        P("groups"),
        P(None, "col"),
        P(None, "col"),
        P(None, "col"),
        P(None, "col"),
        P(None, "col"),
        P(None, "col"),
        P(None, "col"),
        P(),
        P(),
        P(),
        P("col"),
        P("col", None),
        P("col", None),
        P(),
        P(),
        P(),
        P(),
        P(),
    )
    out_specs = (P(("groups", "row"), "col"), P(("groups", "row"), "col", None))
    row_count, col_count = mesh.shape["row"], mesh.shape["col"]

    def chosen(*args):
        head_count = args[14].shape[1]
        if row_count == col_count and head_count % col_count == 0:
            return fast_body(row_count, col_count, *args)
        return body(*args)

    return jax.shard_map(chosen, mesh=mesh, in_specs=in_specs, out_specs=out_specs, check_vma=False)
```

```python
import functools
import math

import jax
import jax.numpy as jnp
from jax import lax
from jax.experimental import pallas as pl
from jax.experimental.pallas import tpu as pltpu
from jax.sharding import PartitionSpec as P

EPSILON = 1e-05
MASKED = -1000000000.0


def broadcast(array, axis, root):
    mine = lax.axis_index(axis) == root
    return lax.psum(jnp.where(mine, array, jnp.zeros_like(array)), axis)


def channel_norm(values, gain):
    row_mean = jnp.mean(values, axis=-1, keepdims=True)
    spread = jnp.mean(values * values, axis=-1, keepdims=True) - row_mean * row_mean
    return (values - row_mean) * lax.rsqrt(spread + EPSILON) * gain


def time_embed(step_index, count):
    halfway = count // 2
    ladder = jnp.arange(halfway).astype(jnp.float32)
    freqs = jnp.exp(-math.log(10000.0) * ladder / halfway)
    angles = step_index[0].astype(jnp.float32) * freqs
    return jnp.concatenate([jnp.sin(angles), jnp.cos(angles)])


def head_scores(query_rows, key_rows, bias_terms, head_count):
    query_heads = query_rows.reshape(query_rows.shape[0], head_count, -1)
    key_heads = key_rows.reshape(key_rows.shape[0], head_count, -1)
    raw = jnp.einsum("qhd,khd->hqk", query_heads, key_heads, preferred_element_type=jnp.float32)
    return raw * query_heads.shape[2] ** (-0.5) + bias_terms


def weighted_values(weights_exp, value_rows, head_count):
    value_heads = value_rows.reshape(value_rows.shape[0], head_count, -1).astype(jnp.float32)
    summed = jnp.einsum("hqk,khd->qhd", weights_exp, value_heads, precision=lax.Precision.HIGHEST)
    return summed.reshape(summed.shape[0], -1)


def divide_heads(summed, totals):
    row_count = summed.shape[0]
    head_count = totals.shape[0]
    return (summed.reshape(row_count, head_count, -1) / totals.T[:, :, None]).reshape(row_count, -1)


def transition(flat, gain, w_in, w_down):
    normed = channel_norm(flat, gain).astype(jnp.bfloat16)
    mixed = jnp.dot(normed, w_in, preferred_element_type=jnp.float32)
    halfway = w_down.shape[0]
    hidden = (jax.nn.silu(mixed[:, :halfway]) * mixed[:, halfway:]).astype(jnp.bfloat16)
    return (flat + jnp.dot(hidden, w_down, preferred_element_type=jnp.float32)).astype(jnp.bfloat16)


def body(
    single,
    pair,
    chain,
    live,
    step_index,
    time_scale,
    time_shift,
    w_query,
    w_key,
    w_value,
    w_gate,
    w_out,
    pair_gain,
    bias_weight,
    chain_bias,
    outer_gain,
    w_left,
    w_right,
    w_outer,
    outer_bias,
    trans_gain,
    w_in,
    w_down,
):
    block_rows = single.shape[0]
    model_width = w_query.shape[0]
    head_count = chain_bias.shape[1]
    row_place = lax.axis_index("row")
    col_place = lax.axis_index("col")
    query_start = row_place * block_rows
    key_start = col_place * block_rows
    chain_query = lax.dynamic_slice_in_dim(chain, query_start, block_rows, 0)
    chain_key = lax.dynamic_slice_in_dim(chain, key_start, block_rows, 0)
    live_query = lax.dynamic_slice_in_dim(live, query_start, block_rows, 0).astype(jnp.float32)
    live_keys = lax.dynamic_slice_in_dim(live, key_start, block_rows, 0)
    single_f = single.astype(jnp.float32)
    totals = lax.psum((jnp.sum(single_f, axis=1), jnp.sum(single_f * single_f, axis=1)), "col")
    row_mean = totals[0] / model_width
    inv_std = lax.rsqrt(totals[1] / model_width - row_mean * row_mean + EPSILON)
    embedded = time_embed(step_index, time_scale.shape[0]).astype(jnp.bfloat16)
    mod_scale = jnp.dot(embedded[None], time_scale, preferred_element_type=jnp.float32)[0]
    mod_shift = jnp.dot(embedded[None], time_shift, preferred_element_type=jnp.float32)[0]
    normed = (
        (single_f - row_mean[:, None]) * inv_std[:, None] * (1.0 + mod_scale) + mod_shift
    ).astype(jnp.bfloat16)
    normed_full = lax.all_gather(normed, "col", axis=1, tiled=True)
    query_part = jnp.dot(normed_full, w_query, preferred_element_type=jnp.float32).astype(
        jnp.bfloat16
    )
    key_part = jnp.dot(normed_full, w_key, preferred_element_type=jnp.float32).astype(jnp.bfloat16)
    value_part = jnp.dot(normed_full, w_value, preferred_element_type=jnp.float32).astype(
        jnp.bfloat16
    )
    gate_part = jnp.dot(normed_full, w_gate, preferred_element_type=jnp.float32).astype(
        jnp.bfloat16
    )
    query_full, key_full, value_full, gate_full = (
        lax.all_gather(query_part, "col", axis=1, tiled=True),
        lax.all_gather(key_part, "col", axis=1, tiled=True),
        lax.all_gather(value_part, "col", axis=1, tiled=True),
        lax.all_gather(gate_part, "col", axis=1, tiled=True),
    )
    key_cols, value_cols = (
        broadcast(key_full, "row", col_place),
        broadcast(value_full, "row", col_place),
    )
    pair_normed = channel_norm(pair.astype(jnp.float32), pair_gain).astype(jnp.bfloat16)
    bias_terms = jnp.einsum(
        "qkc,ch->hqk", pair_normed, bias_weight, preferred_element_type=jnp.float32
    )
    same_chain = chain_query[:, None] == chain_key[None, :]
    chain_terms = jnp.where(
        same_chain[None], chain_bias[0][:, None, None], chain_bias[1][:, None, None]
    )
    live_terms = jnp.where(live_keys == 1, 0.0, MASKED).astype(jnp.float32)
    bias_terms = bias_terms + chain_terms + live_terms[None, None, :]
    scores = head_scores(query_full, key_cols, bias_terms, head_count)
    row_top = lax.pmax(jnp.max(scores, axis=2), "col")
    weights_exp = jnp.exp(scores - row_top[:, :, None])
    row_sum, summed = lax.psum(
        (jnp.sum(weights_exp, axis=2), weighted_values(weights_exp, value_cols, head_count)), "col"
    )
    attended = divide_heads(summed, row_sum)
    gated = (jax.nn.sigmoid(gate_full.astype(jnp.float32)) * attended).astype(jnp.bfloat16)
    single_out = (single_f + jnp.dot(gated, w_out, preferred_element_type=jnp.float32)).astype(
        jnp.bfloat16
    )
    updated_single = single_out.astype(jnp.float32)
    gained = updated_single * outer_gain
    joint = lax.psum(
        (
            jnp.sum(updated_single, axis=1),
            jnp.sum(updated_single * updated_single, axis=1),
            jnp.dot(gained, w_left, precision=lax.Precision.HIGHEST),
            jnp.dot(gained, w_right, precision=lax.Precision.HIGHEST),
            jnp.dot(outer_gain[None], w_left, precision=lax.Precision.HIGHEST)[0],
            jnp.dot(outer_gain[None], w_right, precision=lax.Precision.HIGHEST)[0],
        ),
        "col",
    )
    out_mean = joint[0] / model_width
    out_inv = lax.rsqrt(joint[1] / model_width - out_mean * out_mean + EPSILON)
    left_full = out_inv[:, None] * (joint[2] - out_mean[:, None] * joint[4][None, :])
    right_full = out_inv[:, None] * (joint[3] - out_mean[:, None] * joint[5][None, :])
    left_rows = left_full.astype(jnp.bfloat16)
    right_rows = right_full.astype(jnp.bfloat16)
    right_cols = broadcast(right_rows, "row", col_place)
    left_mix = jnp.einsum("ip,pqc->iqc", left_rows, w_outer, preferred_element_type=jnp.float32)
    outer = (
        jnp.einsum(
            "iqc,jq->ijc", left_mix, right_cols.astype(jnp.float32), precision=lax.Precision.HIGHEST
        )
        + outer_bias
    )
    outer = outer * (live_query[:, None] * live_keys.astype(jnp.float32)[None, :])[:, :, None]
    updated = pair.astype(jnp.float32) + outer
    flat = updated.reshape(-1, updated.shape[-1])
    total_rows = flat.shape[0]
    piece_rows = math.gcd(total_rows, 1024)
    pieces = flat.reshape(total_rows // piece_rows, piece_rows, flat.shape[1])
    pair_out = lax.map(lambda piece: transition(piece, trans_gain, w_in, w_down), pieces).reshape(
        pair.shape
    )
    return (single_out, pair_out)


MESH_ID = pl.DeviceIdType.MESH


def transposed_dot(left, right, precision=None):
    return lax.dot_general(
        left,
        right,
        (((1,), (1,)), ((), ())),
        precision=precision,
        preferred_element_type=jnp.float32,
    )


def pack(values):
    rows, width = values.shape
    whole = width - width % 128
    if rows % 32 or 2 * (width - whole) != 128:
        return values
    half = rows // 2
    rest = jnp.concatenate([values[:half, whole:], values[half:, whole:]], axis=1)
    columns = [values[:, place : place + 128] for place in range(0, whole, 128)]
    return jnp.concatenate(columns + [rest], axis=0)


def unpack(held, rows, width):
    whole = width - width % 128
    if held.shape == (rows, width):
        return held
    rest = held[(whole // 128) * rows :]
    rest = jnp.concatenate([rest[:, :64], rest[:, 64:]], axis=0)
    columns = [held[place * rows : (place + 1) * rows] for place in range(whole // 128)]
    return jnp.concatenate(columns + [rest], axis=1)


def attention_kernel(
    row_count,
    col_count,
    head_size,
    single_ref,
    embedded_ref,
    scale_ref,
    shift_ref,
    chain_ref,
    live_ref,
    pair_gain_ref,
    bias_w_ref,
    chain_bias_ref,
    gain_ref,
    left_w_ref,
    right_w_ref,
    pair_hbm,
    query_w_hbm,
    key_w_hbm,
    value_w_hbm,
    gate_w_hbm,
    out_w_hbm,
    outer_w_hbm,
    single_out_ref,
    mix_ref,
    right_ref,
    pair_ref,
    query_w_ref,
    key_w_ref,
    value_w_ref,
    gate_w_ref,
    out_w_ref,
    outer_w_ref,
    outer_wide,
    outer_flat,
    packed,
    singles,
    mods,
    biases,
    keys_values,
    gates,
    left_parts,
    right_parts,
    own_right,
    load_sem,
    col_send,
    col_recv,
    row_send,
    row_recv,
    right_send,
    right_recv,
):
    row_place = lax.axis_index("row")
    col_place = lax.axis_index("col")
    rows, width = single_ref.shape
    half = rows // 2
    model_width = query_w_ref.shape[1]
    factor = left_w_ref.shape[0]
    head_count = width // head_size
    all_heads = chain_bias_ref.shape[1]
    channels = pair_ref.shape[2]

    def col_peer(step):
        return {"col": lax.rem(col_place + step, col_count)}

    def row_peer(step):
        return {"row": lax.rem(row_place + step, row_count)}

    def copy(source, target, send, recv, device):
        return pltpu.make_async_remote_copy(
            src_ref=source,
            dst_ref=target,
            send_sem=send,
            recv_sem=recv,
            device_id=device,
            device_id_type=MESH_ID,
        )

    loads = [
        pltpu.make_async_copy(source, target, load_sem.at[place])
        for place, (source, target) in enumerate(
            (
                (pair_hbm, pair_ref),
                (key_w_hbm, key_w_ref),
                (value_w_hbm, value_w_ref),
                (query_w_hbm, query_w_ref),
                (gate_w_hbm, gate_w_ref),
                (out_w_hbm, out_w_ref),
                (outer_w_hbm, outer_w_ref),
            )
        )
    ]

    barrier = pltpu.get_barrier_semaphore()
    for row_step in range(row_count):
        for col_step in range(col_count):
            if row_step or col_step:
                pl.semaphore_signal(
                    barrier,
                    inc=1,
                    device_id=row_peer(row_step) | col_peer(col_step),
                    device_id_type=MESH_ID,
                )
    for each in loads:
        each.start()
    embedded = jnp.broadcast_to(embedded_ref[...], (16, embedded_ref.shape[1])).astype(jnp.bfloat16)
    mod_scale = transposed_dot(embedded, scale_ref[...])[:8]
    mod_shift = transposed_dot(embedded, shift_ref[...])[:8]
    mod_row = lax.broadcasted_iota(jnp.int32, mod_scale.shape, 0)
    mods[col_place] = jnp.where(mod_row == 0, mod_scale, mod_shift)
    singles[col_place] = pack(single_ref[...].astype(jnp.float32)).astype(jnp.bfloat16)
    pl.semaphore_wait(barrier, row_count * col_count - 1)

    first = []
    bias_copies = []
    for step in range(1, col_count):
        peer = col_peer(step)
        first.append(
            copy(
                singles.at[col_place],
                singles.at[col_place],
                col_send.at[0, step],
                col_recv.at[0, step],
                peer,
            )
        )
        first.append(
            copy(
                mods.at[col_place],
                mods.at[col_place],
                col_send.at[1, step],
                col_recv.at[1, step],
                peer,
            )
        )
        bias_copies.append(
            copy(
                packed.at[lax.rem(col_place + step, col_count)],
                biases.at[col_place],
                col_send.at[2, step],
                col_recv.at[2, step],
                peer,
            )
        )
    for each in first:
        each.start()
    wide = row_count * rows
    spot = lax.broadcasted_iota(jnp.int32, (rows, wide), 1)
    item = lax.broadcasted_iota(jnp.int32, (rows, wide), 0)
    slot = lax.broadcasted_iota(jnp.int32, (rows, 2 * rows), 1)
    slot = jnp.where(slot >= rows, slot - rows, slot)
    entry = lax.broadcasted_iota(jnp.int32, (rows, 2 * rows), 0)

    def column(row_vector, place):
        picked = jnp.where(spot == item + place * rows, row_vector, 0.0)
        return jnp.sum(picked, axis=1, keepdims=True)

    def twice(column_vector):
        return jnp.sum(jnp.where(slot == entry, column_vector, 0.0), axis=0, keepdims=True)

    chain_all = chain_ref[...].astype(jnp.float32)
    live_all = live_ref[...].astype(jnp.float32)
    live_column = column(live_all, col_place)
    chain_query = column(chain_all, row_place)
    in_first = lax.broadcasted_iota(jnp.int32, (half, 2 * rows), 1) < rows
    chain_packed = jnp.where(in_first, chain_query[:half], chain_query[half:])
    same = chain_packed == twice(column(chain_all, col_place))
    live_term = jnp.where(twice(live_column) == 1.0, 0.0, MASKED)
    loads[0].wait()
    pair_gain = pair_gain_ref[...]
    bias_w = bias_w_ref[...]

    def score_bias(place, carry):
        tile = jnp.concatenate([pair_ref[place], pair_ref[place + half]], axis=0)
        normed = channel_norm(tile.astype(jnp.float32), pair_gain).astype(jnp.bfloat16)
        found = transposed_dot(bias_w, normed)
        for head in range(all_heads):
            packed[
                head // head_count, pl.ds((head % head_count) * half + place, 1), :
            ] = found[head : head + 1]
        return carry

    lax.fori_loop(0, half, score_bias, 0, unroll=4)
    for head in range(all_heads):
        span = pl.ds((head % head_count) * half, half)
        term = jnp.where(
            same, chain_bias_ref[0:1, head : head + 1], chain_bias_ref[1:2, head : head + 1]
        )
        packed[head // head_count, span, :] = packed[head // head_count, span, :] + term + live_term
    for each in bias_copies:
        each.start()
    biases[col_place] = packed[col_place]
    for each in first:
        each.wait()

    gathered = jnp.concatenate(
        [unpack(singles[block].astype(jnp.float32), rows, width) for block in range(col_count)],
        axis=1,
    )
    mod_scale = jnp.concatenate([mods[block, 0:1] for block in range(col_count)], axis=1)
    mod_shift = jnp.concatenate([mods[block, 1:2] for block in range(col_count)], axis=1)
    total = jnp.sum(gathered, axis=1, keepdims=True)
    squares = jnp.sum(gathered * gathered, axis=1, keepdims=True)
    mean = total / model_width
    inv = lax.rsqrt(squares / model_width - mean * mean + EPSILON)
    normed = (gathered - mean) * inv * (1.0 + mod_scale) + mod_shift
    normed = normed.astype(jnp.bfloat16)
    loads[1].wait()
    loads[2].wait()
    key = transposed_dot(normed, key_w_ref[...])
    value = transposed_dot(normed, value_w_ref[...])
    keys_values[row_place, 0] = key.astype(jnp.bfloat16)
    keys_values[row_place, 1] = value.astype(jnp.bfloat16)
    second = [
        copy(
            keys_values.at[row_place],
            keys_values.at[row_place],
            row_send.at[step],
            row_recv.at[step],
            row_peer(step),
        )
        for step in range(1, row_count)
    ]
    for each in second:
        each.start()
    loads[3].wait()
    loads[4].wait()
    query = transposed_dot(normed, query_w_ref[...])
    gate = transposed_dot(normed, gate_w_ref[...])
    opened = jax.nn.sigmoid(gate.astype(jnp.bfloat16).astype(jnp.float32))
    query = query.astype(jnp.bfloat16)
    lane = lax.broadcasted_iota(jnp.int32, (rows, width), 1)
    masks = [
        (lane >= head * head_size) & (lane < (head + 1) * head_size) for head in range(head_count)
    ]
    query_heads = jnp.concatenate(
        [jnp.where(mask, query, jnp.zeros_like(query)) for mask in masks], axis=0
    )
    loads[6].wait()
    outer_wide[...] = outer_w_ref[...].astype(jnp.float32)
    for place in range(factor):
        outer_flat[:, place * channels : (place + 1) * channels] = outer_wide[:, place, :].astype(
            jnp.bfloat16
        )
    for each in bias_copies:
        each.wait()
    for each in second:
        each.wait()

    def unpack_bias(block):
        held = biases[block]
        pieces = []
        for head in range(head_count):
            part = held[head * half : (head + 1) * half]
            pieces += [part[:, :rows], part[:, rows:]]
        return jnp.concatenate(pieces, axis=0)

    scores = [
        transposed_dot(query_heads, keys_values[block, 0]) * head_size ** (-0.5) + unpack_bias(block)
        for block in range(row_count)
    ]
    top = functools.reduce(jnp.maximum, [jnp.max(s, axis=1, keepdims=True) for s in scores])
    weights = [jnp.exp(s - top) for s in scores]
    weight_sum = sum(jnp.sum(w, axis=1, keepdims=True) for w in weights)
    summed = sum(
        jnp.dot(
            weights[block].astype(jnp.bfloat16),
            keys_values[block, 1],
            preferred_element_type=jnp.float32,
        )
        for block in range(row_count)
    )
    summed = summed / weight_sum
    attended = sum(
        jnp.where(masks[head], summed[head * rows : (head + 1) * rows], 0.0)
        for head in range(head_count)
    )
    gates[col_place] = pack(opened * attended).astype(jnp.bfloat16)
    third = [
        copy(
            gates.at[col_place],
            gates.at[col_place],
            col_send.at[3, step],
            col_recv.at[3, step],
            col_peer(step),
        )
        for step in range(1, col_count)
    ]
    for each in third:
        each.start()
    for each in third:
        each.wait()
    loads[5].wait()
    gated = jnp.concatenate(
        [unpack(gates[block].astype(jnp.float32), rows, width) for block in range(col_count)],
        axis=1,
    ).astype(jnp.bfloat16)
    mixed = single_ref[...].astype(jnp.float32) + transposed_dot(gated, out_w_ref[...])
    single_out = mixed.astype(jnp.bfloat16)
    single_out_ref[...] = single_out
    updated = single_out.astype(jnp.float32)
    gain = gain_ref[...]
    precise = lax.Precision.HIGHEST
    factors = jnp.concatenate([left_w_ref[...], right_w_ref[...]], axis=0)
    products = transposed_dot(factors, updated * gain, precise)
    ones = jnp.ones((8, width), jnp.float32)
    totals = jnp.concatenate(
        [
            transposed_dot(ones, updated, precise),
            transposed_dot(ones, updated * updated, precise),
        ],
        axis=1,
    )
    weight_sums = transposed_dot(jnp.broadcast_to(gain, (8, width)), factors, precise)
    weight_sums = jnp.concatenate([weight_sums, jnp.zeros_like(totals[:, 2 * factor :])], axis=1)
    stat_row = lax.broadcasted_iota(jnp.int32, totals.shape, 0)
    statistics = jnp.where(stat_row == 0, totals, weight_sums)
    part = factor // 2
    for parts, start in ((left_parts, 0), (own_right, factor)):
        sides = [products[start : start + part], products[start + part : start + factor]]
        joined = jnp.concatenate([jnp.concatenate(sides, axis=1), statistics], axis=0)
        if parts is left_parts:
            parts[col_place] = joined
        else:
            parts[...] = joined
    fourth = [
        copy(
            left_parts.at[col_place],
            left_parts.at[col_place],
            col_send.at[4, step],
            col_recv.at[4, step],
            col_peer(step),
        )
        for step in range(1, col_count)
    ]
    right_copies = [
        copy(
            own_right,
            right_parts.at[col_place],
            right_send.at[step],
            right_recv.at[col_place],
            row_peer(step) | {"col": row_place},
        )
        for step in range(row_count)
    ]
    diagonal = row_place == col_place
    for step in range(1, row_count):
        right_copies[step].start()

    @pl.when(jnp.logical_not(diagonal))
    def _():
        right_copies[0].start()

    for each in fourth:
        each.start()

    @pl.when(diagonal)
    def _():
        right_parts[col_place] = own_right[...]

    for each in fourth:
        each.wait()

    which_factor = lax.broadcasted_iota(jnp.int32, (factor, 2 * rows), 0)
    which_lane = lax.broadcasted_iota(jnp.int32, (factor, 2 * rows), 1)

    def finish(parts, start):
        joint = parts[0]
        for block in range(1, col_count):
            joint = joint + parts[block]
        out_mean = joint[part : part + 1, :rows] / model_width
        out_square = joint[part : part + 1, rows:] / model_width
        out_inv = lax.rsqrt(out_square - out_mean * out_mean + EPSILON)
        picked = jnp.where(which_lane == which_factor + start, joint[part + 1 : part + 2], 0.0)
        sums = jnp.sum(picked, axis=1, keepdims=True)
        body_rows = jnp.concatenate([joint[:part, :rows], joint[:part, rows:]], axis=0)
        return out_inv * (body_rows - out_mean * sums)

    left = finish(left_parts, 0).T.astype(jnp.bfloat16)
    for which in range(factor):
        mix_ref[:, which, :] = jnp.dot(
            left,
            outer_flat[:, which * channels : (which + 1) * channels],
            preferred_element_type=jnp.float32,
        )
    for block in range(col_count):

        @pl.when(jnp.logical_not(diagonal & (col_place == block)))
        def _():
            copy(
                own_right,
                right_parts.at[block],
                right_send.at[0],
                right_recv.at[block],
                row_peer(0),
            ).wait_recv()

    right = finish(right_parts, factor).astype(jnp.bfloat16).astype(jnp.float32)
    top = jnp.where(lax.broadcasted_iota(jnp.int32, right.shape, 0) == 0, 1.0, 0.0)
    right = jnp.concatenate([top, right, top, right], axis=0).T * live_column
    right_ref[...] = right.astype(jnp.bfloat16)
    for step in range(1, row_count):
        right_copies[step].wait_send()

    @pl.when(jnp.logical_not(diagonal))
    def _():
        right_copies[0].wait_send()


def pair_kernel(
    live_ref,
    pair_ref,
    mix_ref,
    right_ref,
    outer_bias_ref,
    gain_ref,
    w_in_ref,
    w_down_ref,
    out_ref,
    flat_ref,
):
    block_rows, key_rows, channels = pair_ref.shape
    start = lax.axis_index("row") * key_rows + pl.program_id(0) * block_rows
    right = right_ref[...]
    factor = mix_ref.shape[1]
    top = lax.broadcasted_iota(jnp.int32, (factor, channels), 0)
    bias_rows = jnp.where(top == 0, outer_bias_ref[...], 0.0)
    for place in range(block_rows):
        terms = jnp.concatenate([bias_rows, mix_ref[place]], axis=0)
        high = terms.astype(jnp.bfloat16)
        low = (terms - high.astype(jnp.float32)).astype(jnp.bfloat16)
        outer = jnp.dot(
            right,
            jnp.concatenate([high, low], axis=0),
            preferred_element_type=jnp.float32,
        )
        outer = outer * live_ref[start + place].astype(jnp.float32)
        flat_ref[pl.ds(place * key_rows, key_rows), :] = pair_ref[place].astype(jnp.float32) + outer
    flat = flat_ref[...]
    normed = channel_norm(flat, gain_ref[...]).astype(jnp.bfloat16)
    hidden_width = w_down_ref.shape[0]
    chunk = math.gcd(hidden_width, 256)
    result = flat
    for first in range(0, hidden_width, chunk):
        gate = jnp.dot(normed, w_in_ref[:, first : first + chunk], preferred_element_type=jnp.float32)
        up = jnp.dot(
            normed,
            w_in_ref[:, hidden_width + first : hidden_width + first + chunk],
            preferred_element_type=jnp.float32,
        )
        half = gate * 0.5
        hidden = ((half + half * jnp.tanh(half)) * up).astype(jnp.bfloat16)
        result = result + jnp.dot(
            hidden, w_down_ref[first : first + chunk, :], preferred_element_type=jnp.float32
        )
    out_ref[...] = result.astype(jnp.bfloat16).reshape(out_ref.shape)


def fast_body(
    row_count,
    col_count,
    single,
    pair,
    chain,
    live,
    step_index,
    time_scale,
    time_shift,
    w_query,
    w_key,
    w_value,
    w_gate,
    w_out,
    pair_gain,
    bias_weight,
    chain_bias,
    outer_gain,
    w_left,
    w_right,
    w_outer,
    outer_bias,
    trans_gain,
    w_in,
    w_down,
):
    rows, width = single.shape
    model_width = w_query.shape[0]
    head_count = chain_bias.shape[1]
    head_size = model_width // head_count
    local_heads = head_count // col_count
    factor = w_left.shape[1]
    channels = pair.shape[2]
    embedded = time_embed(step_index, time_scale.shape[0]).astype(jnp.bfloat16)
    lanes = 4 * factor
    vmem = pl.BlockSpec(memory_space=pltpu.VMEM)
    bf16, f32 = jnp.bfloat16, jnp.float32
    packed_shape = jax.eval_shape(pack, jax.ShapeDtypeStruct((rows, width), f32)).shape
    hbm = pl.BlockSpec(memory_space=pl.ANY)
    weight = pltpu.VMEM((width, model_width), bf16)
    single_out, mix, right = pl.pallas_call(
        functools.partial(attention_kernel, row_count, col_count, head_size),
        out_shape=(
            jax.ShapeDtypeStruct((rows, width), bf16),
            jax.ShapeDtypeStruct((rows, factor, channels), f32),
            jax.ShapeDtypeStruct((rows, lanes), bf16),
        ),
        in_specs=[vmem] * 12 + [hbm] * 7,
        out_specs=(vmem, vmem, vmem),
        scratch_shapes=[
            pltpu.VMEM(pair.shape, bf16),
            weight,
            weight,
            weight,
            weight,
            weight,
            pltpu.VMEM(w_outer.shape, bf16),
            pltpu.VMEM(w_outer.shape, f32),
            pltpu.VMEM((factor, factor * channels), bf16),
            pltpu.VMEM((col_count, local_heads * rows // 2, 2 * rows), f32),
            pltpu.VMEM((col_count,) + packed_shape, bf16),
            pltpu.VMEM((col_count, 8, width), f32),
            pltpu.VMEM((col_count, local_heads * rows // 2, 2 * rows), f32),
            pltpu.VMEM((row_count, 2, rows, width), bf16),
            pltpu.VMEM((col_count,) + packed_shape, bf16),
            pltpu.VMEM((col_count, factor // 2 + 8, 2 * rows), f32),
            pltpu.VMEM((col_count, factor // 2 + 8, 2 * rows), f32),
            pltpu.VMEM((factor // 2 + 8, 2 * rows), f32),
            pltpu.SemaphoreType.DMA((7,)),
            pltpu.SemaphoreType.DMA((5, col_count)),
            pltpu.SemaphoreType.DMA((5, col_count)),
            pltpu.SemaphoreType.DMA((row_count,)),
            pltpu.SemaphoreType.DMA((row_count,)),
            pltpu.SemaphoreType.DMA((row_count,)),
            pltpu.SemaphoreType.DMA((col_count,)),
        ],
        compiler_params=pltpu.CompilerParams(collective_id=0, has_side_effects=True),
        name="attention",
    )(
        single,
        embedded[None].astype(f32),
        time_scale.T,
        time_shift.T,
        chain[None],
        live[None],
        pair_gain[None],
        bias_weight.T,
        chain_bias,
        outer_gain[None],
        w_left.T,
        w_right.T,
        pair,
        w_query.T,
        w_key.T,
        w_value.T,
        w_gate.T,
        w_out.T,
        w_outer,
    )
    block = math.gcd(rows, 32)
    hidden = w_down.shape[0]
    pair_out = pl.pallas_call(
        pair_kernel,
        grid=(rows // block,),
        out_shape=jax.ShapeDtypeStruct(pair.shape, bf16),
        in_specs=[
            pl.BlockSpec(memory_space=pltpu.SMEM),
            pl.BlockSpec((block, rows, channels), lambda i: (i, 0, 0)),
            pl.BlockSpec((block, factor, channels), lambda i: (i, 0, 0)),
            pl.BlockSpec((rows, lanes), lambda i: (0, 0)),
            pl.BlockSpec((1, channels), lambda i: (0, 0)),
            pl.BlockSpec((1, channels), lambda i: (0, 0)),
            pl.BlockSpec((channels, 2 * hidden), lambda i: (0, 0)),
            pl.BlockSpec((hidden, channels), lambda i: (0, 0)),
        ],
        out_specs=pl.BlockSpec((block, rows, channels), lambda i: (i, 0, 0)),
        scratch_shapes=[pltpu.VMEM((block * rows, channels), f32)],
        name="transition",
    )(
        live,
        pair,
        mix,
        right,
        outer_bias[None],
        trans_gain[None],
        w_in,
        w_down,
    )
    return (single_out, pair_out)


def solution(mesh):
    in_specs = (
        P(("groups", "row"), "col"),
        P(("groups", "row"), "col", None),
        P("groups"),
        P("groups"),
        P("groups"),
        P(None, "col"),
        P(None, "col"),
        P(None, "col"),
        P(None, "col"),
        P(None, "col"),
        P(None, "col"),
        P(None, "col"),
        P(),
        P(),
        P(),
        P("col"),
        P("col", None),
        P("col", None),
        P(),
        P(),
        P(),
        P(),
        P(),
    )
    out_specs = (P(("groups", "row"), "col"), P(("groups", "row"), "col", None))
    row_count, col_count = mesh.shape["row"], mesh.shape["col"]

    def chosen(*args):
        head_count = args[14].shape[1]
        if row_count == col_count and head_count % col_count == 0:
            return fast_body(row_count, col_count, *args)
        return body(*args)

    return jax.shard_map(chosen, mesh=mesh, in_specs=in_specs, out_specs=out_specs, check_vma=False)
```
